128 devices in a mesh: lat: 16 (over x, z_lo, core), lon: 8 (over z_hi, y).
Axes of the slice: x: 4, y: 4, z: 4 (z_hi: 2, z_lo: 2; z = z_hi * 2 + z_lo), core: 2. Of those that a mesh axis runs over, the one named last changes fastest.
Arguments:
- x_tiles: bfloat16 [8, 64, 77, 256], P('lon', 'lat'), may hold values from -6 to 6
- tile_pos: int32 [8, 64], P('lon', 'lat'), may hold values from 0 to 511, as said below
- valid_rows: int32 [8, 64], P('lon', 'lat'), may hold values from 1 to 16
- stem_w: bfloat16 [77, 200], replicated, may hold values from -0.625 to 0.625
- dw_kernel: float32 [200, 49], replicated, may hold values from -0.875 to 0.875
- norm_gain: float32 [200], replicated, may hold values from 0.1 to 1.9
- w_in: bfloat16 [200, 800], replicated, may hold values from -0.4375 to 0.4375
- w_out: bfloat16 [800, 200], replicated, may hold values from -0.21875 to 0.21875
- cotangent: bfloat16 [8, 64, 200, 256], P('lon', 'lat'), may hold values from -3072 to 3072
Outputs:
- out_tiles: bfloat16 [8, 64, 200, 256], P('lon', 'lat')
- grad_w_in: float32 [200, 800], replicated
- grad_w_out: float32 [800, 200], replicated
- grad_kernel: float32 [200, 49], replicated
- grad_gain: float32 [200], replicated
The draws below stay inside these ranges and needn't reach their ends.
Inputs may be any that keep to these rules, and one draw needn't show every extreme that they name: `tile_pos`: in each sector the places are distinct; in the order of place, the r-th active tile of a sector is held by lat index r % 16. At most 2 tiles of one device lie in one band block of 32 tiles, and this is reached; some band block is fully active in every sector.
All inputs are finite; a program needn't handle non-finite values.
Results may differ from the reference program's by a relative error of at most 0.0075.
Values may be sent and summed in bfloat16 or wider, within the bound.
No kernel may reach another device: no remote copies, remote signals or barrier semaphores. Data moves between devices by JAX's collectives and lax.ppermute only.
A program may use at most 128 MiB of HBM per device.

```python
import jax
import jax.numpy as jnp
from jax import lax

C = 200
CIN = 77
HID = 800
KW = 7
TS = 16
BH = 64
BW = 128
A_DEV = 4
TT = 256
K_TILES = 32
ACT = 64
N_LAT = 16
N_LON = 8


def draw_tile_pos(key, part):
    tiles_all = K_TILES * N_LAT
    picked = A_DEV * N_LAT

    def one_sector(sector_key):
        base_key, band_key, full_key = jax.random.split(sector_key, 3)
        tile_index = jnp.arange(tiles_all, dtype=jnp.int32)
        band_of = tile_index // K_TILES
        base_score = jax.random.randint(base_key, (tiles_all,), 0, 4096)
        band_bias = jax.random.randint(band_key, (N_LAT,), 0, 8192)
        full_band = jax.random.randint(full_key, (), 0, N_LAT)
        forced = jnp.where((band_of == full_band) | (tile_index == 0) | (tile_index == tiles_all - 1), 16384, 0)
        score_all = (base_score + band_bias[band_of] + forced) * tiles_all + tile_index
        chosen = jnp.sort(lax.top_k(score_all, picked)[1])
        return chosen.reshape(A_DEV, N_LAT).T.reshape(picked).astype(jnp.int32)
    sector_keys = jax.random.split(key, N_LON)
    return jax.vmap(one_sector)(sector_keys)


def draw_valid_rows(key, part):
    drawn = jax.random.randint(key, (N_LON, A_DEV * N_LAT), 1, TS + 1)
    drawn = drawn.at[:, 0].set(TS)
    return drawn.at[:, 1].set(1).astype(jnp.int32)


def block_scale(stream_key, dims, shards, least, top_value):
    factor_of = 1.0
    for position, shards_of in shards:
        heights = jax.random.uniform(jax.random.fold_in(jax.random.fold_in(stream_key, 6), position), (shards_of,), jnp.float32, least / len(shards), top_value / len(shards))
        factor_of = factor_of * jnp.repeat(jnp.exp(heights), dims[position] // shards_of).reshape((-1,) + (1,) * (len(dims) - 1 - position))
    return factor_of


def bell_draw(stream_key, shape, deviation, most, pieces=(), held_as=jnp.bfloat16):
    entries = jax.random.normal(stream_key, shape, jnp.float32) * deviation
    if len(pieces) > 0:
        entries = block_scale(stream_key, shape, pieces, -0.22, 0.18) * entries
    return jnp.clip(entries, min=-most, max=most).astype(held_as)


def setup_inputs(seed: int = 0) -> dict:
    key_list = jax.random.split(jax.random.key(seed), 10)
    x_tiles = bell_draw(key_list[0], (N_LON, ACT, CIN, TT), 1.0, 6.0, ((0, 8), (1, 16)))
    tile_pos = draw_tile_pos(jax.random.fold_in(key_list[9], 71), 0)
    valid_rows = draw_valid_rows(jax.random.fold_in(key_list[9], 71), 0)
    stem_w = bell_draw(key_list[3], (CIN, C), CIN ** -0.5, 0.625)
    dw_kernel = bell_draw(key_list[4], (C, KW * KW), (KW * KW) ** -0.5, 0.875, (), jnp.float32)
    norm_gain = jnp.clip(1.0 + 0.18 * jax.random.normal(key_list[5], (C,), jnp.float32), 0.1, 1.9)
    w_in = bell_draw(key_list[6], (C, HID), C ** -0.5, 0.4375)
    w_out = bell_draw(key_list[7], (HID, C), HID ** -0.5, 0.21875)
    cotangent = bell_draw(key_list[8], (N_LON, ACT, C, TT), 512.0, 3072.0, ((0, 8), (1, 16)))
    return {"x_tiles": x_tiles, "tile_pos": tile_pos, "valid_rows": valid_rows, "stem_w": stem_w, "dw_kernel": dw_kernel, "norm_gain": norm_gain, "w_in": w_in, "w_out": w_out, "cotangent": cotangent}


def gelu_tanh(value):
    return jax.nn.gelu(value, approximate=True)

def to_grid(grid_tiles):
    chan = grid_tiles.shape[2]
    shaped = grid_tiles.reshape(N_LON, N_LAT, BH // TS, BW // TS, chan, TS, TS)
    return shaped.transpose(4, 1, 2, 5, 0, 3, 6).reshape(chan, BH * N_LAT, BW * N_LON)

def from_grid(grid):
    chan = grid.shape[0]
    shaped = grid.reshape(chan, N_LAT, BH // TS, TS, N_LON, BW // TS, TS)
    return shaped.transpose(4, 1, 2, 5, 0, 3, 6).reshape(N_LON, N_LAT * K_TILES, chan, TS * TS)

def place_tiles(values, tile_pos):
    sector_ids = jnp.arange(N_LON, dtype=jnp.int32)[:, None]
    empty = jnp.zeros((N_LON, N_LAT * K_TILES, values.shape[2], TS * TS), values.dtype)
    return to_grid(empty.at[sector_ids, tile_pos].set(values))

def pick_tiles(grid, tile_pos):
    sector_ids = jnp.arange(N_LON, dtype=jnp.int32)[:, None]
    return from_grid(grid)[sector_ids, tile_pos]

def band_rows(lat_pad, band_index):
    reach = KW // 2
    start = (band_index * BH).astype(jnp.int32)
    rows = lax.dynamic_slice_in_dim(lat_pad, start, BH + 2 * reach, axis=1)
    return jnp.concatenate([rows[:, :, -reach:], rows, rows[:, :, :reach]], axis=2)

def band_norm(padded, dw_kernel):
    width = padded.shape[2] - 2 * (KW // 2)
    conv_out = jnp.zeros((padded.shape[0], BH, width), jnp.float32)
    for tap_index in range(KW * KW):
        row_off = tap_index // KW
        col_off = tap_index % KW
        conv_out = conv_out + dw_kernel[:, tap_index][:, None, None] * padded[:, row_off:row_off + BH, col_off:col_off + width].astype(jnp.float32)
    centred = conv_out - lax.optimization_barrier(jnp.mean(conv_out, axis=0, keepdims=True))
    inv_std = lax.rsqrt(lax.optimization_barrier(jnp.mean(centred * centred, axis=0, keepdims=True)) + 1e-06)
    return (centred * inv_std, inv_std)

def stack_bands(banded):
    chan = banded.shape[1]
    return banded.transpose(1, 0, 2, 3).reshape(chan, N_LAT * BH, banded.shape[3])

def reference(x_tiles, tile_pos, valid_rows, stem_w, dw_kernel, norm_gain, w_in, w_out, cotangent):
    f32 = jnp.float32
    bf16 = jnp.bfloat16
    reach = KW // 2
    cell_rows = jnp.arange(TS * TS, dtype=jnp.int32) // TS
    ocean_mask = (cell_rows[None, None, :] < valid_rows[:, :, None]).astype(f32)
    stem_tiles = (jnp.einsum('kc,sakp->sacp', stem_w.astype(f32), x_tiles.astype(f32)) * ocean_mask[:, :, None, :]).astype(bf16)
    band_grid = place_tiles(stem_tiles, tile_pos)
    lat_pad = jnp.pad(band_grid, ((0, 0), (reach, reach), (0, 0)))
    band_ids = jnp.arange(N_LAT, dtype=jnp.int32)

    def forward_band(band_index):
        unit, inv_std = band_norm(band_rows(lat_pad, band_index), dw_kernel)
        return (unit * norm_gain[:, None, None]).astype(bf16)
    normed = stack_bands(lax.map(forward_band, band_ids))
    features = pick_tiles(normed, tile_pos)

    def sector_work(items):
        feats, stems, upstream, mask_s = items
        preact = jnp.einsum('ch,acp->ahp', w_in.astype(f32), feats.astype(f32))
        hidden = gelu_tanh(preact).astype(bf16)
        branch = jnp.einsum('hc,ahp->acp', w_out.astype(f32), hidden.astype(f32))
        result = (mask_s[:, None, :] * (stems.astype(f32) + branch)).astype(bf16)
        masked_grad = (upstream.astype(f32) * mask_s[:, None, :]).astype(bf16)
        grad_hidden = jnp.einsum('hc,acp->ahp', w_out.astype(f32), masked_grad.astype(f32))
        grad_preact = jax.vjp(gelu_tanh, preact)[1](grad_hidden)[0].astype(bf16)
        grad_feats = jnp.einsum('ch,ahp->acp', w_in.astype(f32), grad_preact.astype(f32)).astype(bf16)
        part_in = jnp.einsum('acp,ahp->ch', feats.astype(f32), grad_preact.astype(f32))
        part_out = jnp.einsum('ahp,acp->hc', hidden.astype(f32), masked_grad.astype(f32))
        return (result, grad_feats, part_in, part_out)
    out_tiles, grad_features, parts_in, parts_out = lax.map(sector_work, (features, stem_tiles, cotangent, ocean_mask))
    grad_grid = place_tiles(grad_features, tile_pos)

    def backward_band(band_index):
        padded = band_rows(lat_pad, band_index)
        unit, inv_std = band_norm(padded, dw_kernel)
        start = (band_index * BH).astype(jnp.int32)
        grad_band = lax.dynamic_slice_in_dim(grad_grid, start, BH, axis=1).astype(f32)
        scaled = grad_band * norm_gain[:, None, None]
        grad_conv = inv_std * (scaled - lax.optimization_barrier(jnp.mean(scaled, axis=0, keepdims=True)) - unit * lax.optimization_barrier(jnp.mean(scaled * unit, axis=0, keepdims=True)))
        width = grad_band.shape[2]
        kernel_terms = []
        for tap_index in range(KW * KW):
            row_off = tap_index // KW
            col_off = tap_index % KW
            kernel_terms.append(lax.optimization_barrier(jnp.sum(grad_conv * padded[:, row_off:row_off + BH, col_off:col_off + width].astype(f32), axis=(1, 2))))
        return (jnp.stack(kernel_terms, axis=1), lax.optimization_barrier(jnp.sum(grad_band * unit, axis=(1, 2))))
    kernel_parts, gain_parts = lax.map(backward_band, band_ids)
    cell_total = TS * jnp.sum(valid_rows.astype(f32))
    grad_kernel = lax.optimization_barrier(jnp.sum(kernel_parts, axis=0)) / cell_total
    grad_gain = lax.optimization_barrier(jnp.sum(gain_parts, axis=0)) / cell_total
    grad_w_in = lax.optimization_barrier(jnp.sum(parts_in, axis=0)) / cell_total
    grad_w_out = lax.optimization_barrier(jnp.sum(parts_out, axis=0)) / cell_total
    return (out_tiles, grad_w_in, grad_w_out, grad_kernel, grad_gain)
```

```python
import jax
import jax.numpy as jnp
import numpy as np
from jax import lax
from jax.experimental import pallas as pl
from jax.experimental.pallas import tpu as pltpu
from jax.sharding import PartitionSpec as P

C = 200
CIN = 77
HID = 800
KW = 7
TS = 16
TT = 256
A_DEV = 4
COLS = 8
TILE_ROWS = 64
HALF = 128
KPAD = 80
PIECE = 48
SHELL = 4 * PIECE
EDGE = A_DEV * PIECE
PAY = A_DEV * SHELL + 2 * EDGE
GROUP = 8
PITCH = 24
PROWS = TS + KW - 1
HB = 7
CHUNKS = 64
F32 = jnp.float32
BF16 = jnp.bfloat16
TN = (((0,), (0,)), ((), ()))
NT = (((1,), (1,)), ((), ()))
DIRS = [(dr, dc) for dr in (-1, 0, 1) for dc in (-1, 0, 1) if (dr, dc) != (0, 0)]


def shell_cells():
    m = np.arange(PIECE)
    left = (m // 3) * TS + m % 3
    pieces = np.concatenate([m, 13 * TS + m, left, left + 13, np.full(256 - SHELL, -1)])
    return pieces.reshape(1, 256).astype(np.int32)


def shell_kernel(pos_ref, rows_ref, x_ref, map_ref, shell_ref, east_ref, west_ref, kept_ref, flat, cut, buf):
    for k in range(CIN):
        for h in range(2):
            flat[h, A_DEV * k : A_DEV * k + A_DEV, :] = x_ref[k, :, h * HALF : (h + 1) * HALF].astype(F32)
    row = lax.broadcasted_iota(jnp.int32, (A_DEV * CIN, 1), 0) % A_DEV
    limit = jnp.full((A_DEV * CIN, 1), rows_ref[0, 0], jnp.int32)
    for a in range(1, A_DEV):
        limit = jnp.where(row == a, rows_ref[0, a], limit)
    cell_row = lax.broadcasted_iota(jnp.int32, (1, TT), 1) // TS
    for h in range(2):
        flat[h] = jnp.where(cell_row[:, h * HALF : (h + 1) * HALF] < limit, flat[h], 0.0)
    cell_id = lax.broadcasted_iota(jnp.int32, (TT, 256), 0)
    pick = (cell_id == map_ref[...]).astype(F32).astype(BF16)
    pieces = jnp.dot(flat[0].astype(BF16), pick[0:HALF], preferred_element_type=F32)
    pieces = pieces + jnp.dot(flat[1].astype(BF16), pick[HALF:TT], preferred_element_type=F32)
    cut[0] = pieces[:, 0:HALF]
    cut[1] = pieces[:, HALF:256]
    fill = lax.broadcasted_iota(jnp.int32, (3, 1), 0)
    buf[:, 768:1536] = jnp.zeros((KPAD, 768), F32)
    kept_ref[...] = jnp.zeros_like(kept_ref)
    for a in range(A_DEV):
        for h in range(2):
            kept_ref[a, 0:CIN, h * HALF : (h + 1) * HALF] = flat[h, pl.ds(a, CIN, stride=A_DEV), :].astype(BF16)
        v0 = cut[0, pl.ds(a, CIN, stride=A_DEV), :]
        v1 = cut[1, pl.ds(a, CIN, stride=A_DEV), :]
        place = pos_ref[0, a]
        tail = jnp.where(fill == 0, place // 16, jnp.where(fill == 1, place % 16, 0)).astype(F32)
        at = a * SHELL
        buf[0:CIN, at : at + HALF] = v0
        buf[0:CIN, at + HALF : at + SHELL] = v1[:, 0 : SHELL - HALF]
        buf[CIN:KPAD, at : at + SHELL] = jnp.broadcast_to(tail, (3, SHELL))
        east = 768 + a * PIECE
        west = 1152 + EDGE + a * PIECE
        buf[0:CIN, east : east + PIECE] = v1[:, 16:64]
        buf[CIN:KPAD, east : east + PIECE] = jnp.broadcast_to(tail, (3, PIECE))
        buf[0:CIN, west : west + 32] = v0[:, 96:HALF]
        buf[0:CIN, west + 32 : west + PIECE] = v1[:, 0:16]
        buf[CIN:KPAD, west : west + PIECE] = jnp.broadcast_to(tail, (3, PIECE))
    shell_ref[...] = buf[:, 0:768].astype(BF16)
    east_ref[...] = buf[:, 768:1152].astype(BF16)
    west_ref[...] = buf[:, 1152:1536].astype(BF16)


def gelu_parts(v):
    k = 0.7978845608028654
    sq = v * v
    u = 0.5 * jnp.tanh(v * (k + (k * 0.044715) * sq)) + 0.5
    value = v * u
    slope = u + (value - value * u) * (2.0 * k + (6.0 * k * 0.044715) * sq)
    return value, slope


def main_kernel(
    pos_ref, rows_ref, core_ref, ga_ref, gb_ref, x_ref, sw_ref, dw_ref, gain_ref, wi_ref, wo_ref, cot_ref,
    out_ref, own_ref, send_ref,
    swp, dwt, gnp, wide, wit, wot, pm, tv, sm, ts, sem, lp, st, pt, cv, un, iv, ft, mg, hs, gps, gf, gc, si, so,
):
    swp[...] = jnp.zeros_like(swp)
    swp[0:CIN, 0:C] = sw_ref[...]
    dwt[1] = jnp.zeros((56, HALF), F32)
    dwt[0, 0 : KW * KW, :] = dw_ref[:, 0:HALF]
    dwt[1, 0 : KW * KW, 0 : C - HALF] = dw_ref[:, HALF:C]
    gnp[...] = jnp.zeros_like(gnp)
    gnp[:, 0:C] = gain_ref[...]
    gain0 = gnp[:, 0:HALF]
    gain1 = gnp[:, HALF:256]

    for g in range(GROUP):
        for j, ref in enumerate((ga_ref, gb_ref)):
            tail = ref[g, 64:KPAD, :].astype(F32)
            pm[2 * g + j : 2 * g + j + 1, :] = tail[13:14, :] * 16.0 + tail[14:15, :]
    lane = lax.broadcasted_iota(jnp.int32, (16, PAY), 1)
    slot = lax.broadcasted_iota(jnp.int32, (16, PAY), 0)
    kind = jnp.where(lane < 768, 0, jnp.where(lane < 768 + EDGE, 1, 2))
    first = jnp.where(lane < 768, lane % SHELL, (lane - 768) % PIECE) == 0
    label = jnp.where(first, pm[...] + 1000.0 * kind.astype(F32), -1.0)
    code = (slot * PAY + lane + 1).astype(F32)
    for a in range(A_DEV):
        q = pos_ref[0, a]
        row, col = q // COLS, q % COLS
        for n, (dr, dc) in enumerate(DIRS):
            nrow, ncol = row + dr, col + dc
            inside = (nrow >= 0) & (nrow < TILE_ROWS)
            side = jnp.where(ncol < 0, 1000, jnp.where(ncol >= COLS, 2000, 0))
            want = jnp.where(inside, nrow * COLS + (ncol + COLS) % COLS + side, -7)
            hit = jnp.where(label == want.astype(F32), code, 0.0)
            acc = jnp.sum(hit, axis=0, keepdims=True)
            folded = acc[:, 0:HALF]
            for i in range(1, PAY // HALF):
                folded = folded + acc[:, i * HALF : (i + 1) * HALF]
            tv[a * 8 + n : a * 8 + n + 1, :] = folded
    total = jnp.sum(tv[...], axis=1, keepdims=True)
    sm[...] = jnp.broadcast_to(total, (32, HALF)).astype(jnp.int32)
    tcopy = pltpu.make_async_copy(sm, ts, sem)
    tcopy.start()

    for a in range(A_DEV):
        rows = lax.dot_general(x_ref[a], swp[...], TN, preferred_element_type=F32)
        rows = rows.astype(BF16).astype(F32)
        for h in range(2):
            for y in range(TS):
                at = (a * PROWS + 3 + y) * PITCH + 3
                pt[h, at : at + TS, :] = rows[y * TS : (y + 1) * TS, h * HALF : (h + 1) * HALF]
    cell_row = lax.broadcasted_iota(jnp.int32, (1, TT), 1) // TS
    mg[...] = jnp.zeros_like(mg)
    for a in range(A_DEV):
        keep = cell_row < rows_ref[0, a]
        mg[0:C, a * TT : (a + 1) * TT] = jnp.where(keep, cot_ref[a].astype(F32), 0.0).astype(BF16)
    wide[C:256, :] = jnp.zeros((256 - C, HB * HALF), F32)
    wide[:, 768:896] = jnp.zeros((256, HALF), F32)
    for src, dst in ((wi_ref, wit), (wo_ref, wot)):
        wide[0:C, 0:HID] = src[...].astype(F32)
        for b in range(HB):
            dst[b * HALF : (b + 1) * HALF, :] = wide[:, b * HALF : (b + 1) * HALF].T.astype(BF16)
    tcopy.wait()

    gap = lax.broadcasted_iota(jnp.int32, (PIECE, 256), 1) - lax.broadcasted_iota(jnp.int32, (PIECE, 256), 0)
    for a in range(A_DEV):
        col = pos_ref[0, a] % COLS
        for n, (dr, dc) in enumerate(DIRS):
            got = ts[a * 8 + n, 0]
            if dc == 0:
                offset = 48 if dr < 0 else 0
            elif dc < 0:
                offset = jnp.where(col == 0, 0, 144)
            else:
                offset = jnp.where(col == COLS - 1, 0, 96)
            spot = jnp.maximum(got - 1, 0)
            source = spot // PAY
            at = spot - source * PAY + offset
            block = jnp.minimum(at // HALF, PAY // HALF - 2)
            shift = jnp.where(got == 0, -1000, at - block * HALF)
            cells = pl.ds(pl.multiple_of(block * HALF, HALF), 256)
            near = ga_ref[source // 2, :, cells]
            far = gb_ref[source // 2, :, cells]
            window = jnp.where(source % 2 == 0, near, far)
            pick = (gap == shift).astype(F32).astype(BF16)
            piece = lax.dot_general(pick, window, NT, preferred_element_type=F32)
            spot = (a * 8 + n) * PIECE
            lp[spot : spot + PIECE, 0:KPAD] = piece.astype(BF16)
    for a in range(A_DEV):
        span = slice(a * 8 * PIECE, (a + 1) * 8 * PIECE)
        rows = jnp.dot(lp[span, 0:KPAD], swp[...], preferred_element_type=F32)
        rows = rows.astype(BF16).astype(F32)
        st[0, span, :] = rows[:, 0:HALF]
        st[1, span, :] = rows[:, HALF:256]
    for a in range(A_DEV):
        base = {where: (a * 8 + n) * PIECE for n, where in enumerate(DIRS)}
        for h in range(2):
            for i in range(3):
                at = (a * PROWS + i) * PITCH
                low = at + 19 * PITCH
                up, down = base[-1, 0] + i * TS, base[1, 0] + i * TS
                pt[h, at + 3 : at + 3 + TS, :] = st[h, up : up + TS, :]
                pt[h, low + 3 : low + 3 + TS, :] = st[h, down : down + TS, :]
                for dc, xx in ((-1, 0), (1, 19)):
                    up, down = base[-1, dc] + 39 + 3 * i, base[1, dc] + 3 * i
                    pt[h, at + xx : at + xx + 3, :] = st[h, up : up + 3, :]
                    pt[h, low + xx : low + xx + 3, :] = st[h, down : down + 3, :]
            for y in range(TS):
                at = (a * PROWS + 3 + y) * PITCH
                for dc, xx in ((-1, 0), (1, 19)):
                    side = base[0, dc] + 3 * y
                    pt[h, at + xx : at + xx + 3, :] = st[h, side : side + 3, :]

    def conv_step(step, carry):
        h = step // (2 * A_DEV)
        part = step % (2 * A_DEV)
        at = pl.multiple_of((part // 2) * (PROWS * PITCH) + (part % 2) * (8 * PITCH), 8)
        acc = [jnp.zeros((TS, HALF), F32) for _ in range(8)]
        for r in range(KW):
            for k in range(KW):
                w = jnp.broadcast_to(dwt[h, r * KW + k : r * KW + k + 1, :], (TS, HALF))
                for y in range(8):
                    acc[y] = acc[y] + w * pt[h, pl.ds(at + (y + r) * PITCH + k, TS), :]
        for y in range(8):
            cv[h, pl.ds(pl.multiple_of(part * HALF, 8) + y * TS, TS), :] = acc[y]
        return carry

    lax.fori_loop(0, 4 * A_DEV, conv_step, 0)

    live = lax.broadcasted_iota(jnp.int32, (1, HALF), 1) < C - HALF
    for a in range(A_DEV):
        span = slice(a * TT, (a + 1) * TT)
        c0 = cv[0, span, :]
        c1 = cv[1, span, :]
        mean = jnp.sum(c0 + c1, axis=1, keepdims=True) * (1.0 / C)
        c0 = c0 - mean
        c1 = jnp.where(live, c1 - mean, 0.0)
        inv = lax.rsqrt(jnp.sum(c0 * c0 + c1 * c1, axis=1, keepdims=True) * (1.0 / C) + 1e-6)
        u0 = c0 * inv
        u1 = c1 * inv
        cv[0, span, :] = u0
        cv[1, span, :] = u1
        iv[span, :] = jnp.broadcast_to(inv, (TT, HALF))
        ft[0:HALF, span] = (u0 * gain0).T.astype(BF16)
        ft[HALF:256, span] = (u1 * gain1).T.astype(BF16)

    for b in range(HID // 80):
        span = slice(b * 80, (b + 1) * 80)
        preact = jnp.dot(wit[span, :], ft[...], preferred_element_type=F32)
        grad_hidden = jnp.dot(wot[span, :], mg[...], preferred_element_type=F32)
        value, slope = gelu_parts(preact)
        hs[span, :] = value.astype(BF16)
        gps[span, :] = (grad_hidden * slope).astype(BF16)
    gf[C:256, :] = jnp.zeros((256 - C, TT), F32)
    sums = [jnp.zeros((1, HALF), F32), jnp.zeros((1, HALF), F32)]
    for a in range(A_DEV):
        span = slice(a * TT, (a + 1) * TT)
        gf[0:C, :] = jnp.dot(wi_ref[...], gps[:, span], preferred_element_type=F32)
        g0 = gf[0:HALF, :].T.astype(BF16).astype(F32)
        g1 = gf[HALF:256, :].T.astype(BF16).astype(F32)
        u0 = cv[0, span, :]
        u1 = cv[1, span, :]
        inv = iv[span, :]
        sums[0] = sums[0] + jnp.sum(g0 * u0, axis=0, keepdims=True)
        sums[1] = sums[1] + jnp.sum(g1 * u1, axis=0, keepdims=True)
        d0 = g0 * gain0
        d1 = g1 * gain1
        m1 = jnp.sum(d0 + d1, axis=1, keepdims=True) * (1.0 / C)
        m2 = jnp.sum(d0 * u0 + d1 * u1, axis=1, keepdims=True) * (1.0 / C)
        gc[0, span, :] = inv * (d0 - m1 - u0 * m2)
        gc[1, span, :] = jnp.where(live, inv * (d1 - m1 - u1 * m2), 0.0)
        stem = lax.dot_general(swp[...], x_ref[a], TN, preferred_element_type=F32)[0:C, :].astype(BF16).astype(F32)
        branch = jnp.dot(wo_ref[...], hs[:, span], preferred_element_type=F32)
        keep = cell_row < rows_ref[0, a]
        out_ref[a] = jnp.where(keep, branch + stem, 0.0).astype(BF16)
    si[:, 768:896] = jnp.zeros((C, HALF), F32)
    so[:, 768:896] = jnp.zeros((C, HALF), F32)
    si[:, 0:HID] = lax.dot_general(ft[0:C, :], gps[...], NT, preferred_element_type=F32)
    so[:, 0:HID] = lax.dot_general(mg[0:C, :], hs[...], NT, preferred_element_type=F32)

    un[0, 48:56, :] = jnp.zeros((8, HALF), F32)
    un[1, 48:56, :] = jnp.zeros((8, HALF), F32)

    def tap_step(step, carry):
        h = step % 2
        r = step // 2
        down = pl.multiple_of(r * PITCH, 8)
        acc = [jnp.zeros((TS, HALF), F32) for _ in range(KW)]
        for a in range(A_DEV):
            for y in range(TS):
                g = gc[h, a * TT + y * TS : a * TT + (y + 1) * TS, :]
                for k in range(KW):
                    acc[k] = acc[k] + g * pt[h, pl.ds(down + (a * PROWS + y) * PITCH + k, TS), :]
        for k in range(KW):
            un[h, pl.ds(r * KW + k, 1), :] = jnp.sum(acc[k], axis=0, keepdims=True)
        return carry

    lax.fori_loop(0, 2 * KW, tap_step, 0)
    un[0, 49:50, :] = sums[0]
    un[1, 49:50, :] = sums[1]

    is_low = core_ref[0, 0] == 0
    blank = jnp.zeros((8, HALF), F32)
    count = ((rows_ref[0, 0] + rows_ref[0, 1] + rows_ref[0, 2] + rows_ref[0, 3]) * TS).astype(F32)

    def blocks(t):
        if t < 25 * HB:
            r, b = t // HB, t % HB
            return si[8 * r : 8 * r + 8, b * HALF : (b + 1) * HALF], so[8 * r : 8 * r + 8, b * HALF : (b + 1) * HALF]
        t = t - 25 * HB
        if t < 14:
            return un[t // HB, 8 * (t % HB) : 8 * (t % HB) + 8, :], blank
        if t == 14:
            return jnp.where(lax.broadcasted_iota(jnp.int32, (8, HALF), 1) == core_ref[0, 1], count, blank), blank
        return blank, blank

    for chunk in range(CHUNKS):
        pairs = [blocks(3 * chunk + i) for i in range(3)]
        for i, (low, high) in enumerate(pairs):
            own_ref[chunk, 8 * i : 8 * i + 8, :] = jnp.where(is_low, low, high)
        sent = jnp.concatenate([jnp.where(is_low, high, low) for low, high in pairs], axis=0)
        send_ref[chunk] = sent.astype(BF16)


def final_kernel(core_ref, own_ref, other_ref, win_ref, wout_ref, ker_ref, gain_ref, ks):
    is_low = core_ref[0, 0] == 0

    def pair(chunk):
        own = own_ref[chunk].astype(F32)
        other = other_ref[chunk].astype(F32)
        return jnp.where(is_low, own, other), jnp.where(is_low, other, own)

    scale = 1.0 / jnp.sum(pair(CHUNKS - 1)[0][0:1, :], axis=1, keepdims=True)
    for chunk in range(CHUNKS - 1):
        low, high = pair(chunk)
        for i in range(3):
            t = 3 * chunk + i
            block = low[8 * i : 8 * i + 8, :] * scale
            if t < 25 * HB:
                r, b = t // HB, t % HB
                wide = HALF if b < HB - 1 else HID - (HB - 1) * HALF
                win_ref[8 * r : 8 * r + 8, b * HALF : b * HALF + wide] = block[:, 0:wide]
                turned = high[8 * i : 8 * i + 8, :] * scale
                wout_ref[8 * r : 8 * r + 8, b * HALF : b * HALF + wide] = turned[:, 0:wide]
            else:
                t = t - 25 * HB
                ks[8 * (t % HB) : 8 * (t % HB) + 8, (t // HB) * HALF : (t // HB + 1) * HALF] = block
    ker_ref[...] = ks[0 : KW * KW, 0:C]
    gain_ref[...] = ks[49:50, 0:C]


def on_chip(value):
    return pltpu.with_memory_space_constraint(value, pltpu.VMEM)


def body(x_tiles, tile_pos, valid_rows, stem_w, dw_kernel, norm_gain, w_in, w_out, cotangent):
    smem = pl.BlockSpec(memory_space=pltpu.SMEM)
    vmem = pl.BlockSpec(memory_space=pltpu.VMEM)
    lat_id = lax.axis_index("lat")
    core_id = jnp.stack([lat_id & 1, lat_id * lax.axis_size("lon") + lax.axis_index("lon")]).reshape(1, 2)
    shell, east, west, inputs = pl.pallas_call(
        shell_kernel,
        out_shape=(
            jax.ShapeDtypeStruct((KPAD, 768), BF16),
            jax.ShapeDtypeStruct((KPAD, 384), BF16),
            jax.ShapeDtypeStruct((KPAD, 384), BF16),
            jax.ShapeDtypeStruct((A_DEV, KPAD, TT), BF16),
        ),
        in_specs=[smem, smem, vmem, vmem],
        out_specs=(vmem, vmem, vmem, vmem),
        scratch_shapes=[
            pltpu.VMEM((2, A_DEV * CIN, HALF), F32),
            pltpu.VMEM((2, A_DEV * CIN, HALF), F32),
            pltpu.VMEM((KPAD, 1536), F32),
        ],
        name="shell",
    )(tile_pos, valid_rows, x_tiles[0].transpose(1, 0, 2), jnp.asarray(shell_cells()))
    lon = lax.axis_size("lon")
    lat = lax.axis_size("lat")
    from_west = lax.ppermute(east, "lon", [(i, (i + 1) % lon) for i in range(lon)])
    from_east = lax.ppermute(west, "lon", [((i + 1) % lon, i) for i in range(lon)])
    payload = jnp.concatenate([shell, from_west + from_east], axis=1)
    same_core = [[i for i in range(c, lat, 2)] for c in range(2)]
    siblings = [(i, i ^ 1) for i in range(lat)]
    mine = lax.all_to_all(
        jnp.broadcast_to(payload[None], (GROUP, KPAD, PAY)), "lat", 0, 0, axis_index_groups=same_core, tiled=True
    )
    theirs = lax.ppermute(mine, "lat", siblings)

    cells = A_DEV * TT
    out_tiles, own, send = pl.pallas_call(
        main_kernel,
        out_shape=(
            jax.ShapeDtypeStruct((A_DEV, C, TT), BF16),
            jax.ShapeDtypeStruct((CHUNKS, 24, HALF), F32),
            jax.ShapeDtypeStruct((CHUNKS, 24, HALF), BF16),
        ),
        in_specs=[smem] * 3 + [vmem] * 9,
        out_specs=(vmem, vmem, vmem),
        scratch_shapes=[
            pltpu.VMEM((KPAD, 256), BF16),
            pltpu.VMEM((2, 56, HALF), F32),
            pltpu.VMEM((1, 256), F32),
            pltpu.VMEM((256, HB * HALF), F32),
            pltpu.VMEM((HB * HALF, 256), BF16),
            pltpu.VMEM((HB * HALF, 256), BF16),
            pltpu.VMEM((16, PAY), F32),
            pltpu.VMEM((32, HALF), F32),
            pltpu.VMEM((32, HALF), jnp.int32),
            pltpu.SMEM((32, HALF), jnp.int32),
            pltpu.SemaphoreType.DMA,
            pltpu.VMEM((32 * PIECE, HALF), BF16),
            pltpu.VMEM((2, 32 * PIECE, HALF), F32),
            pltpu.VMEM((2, A_DEV * PROWS * PITCH, HALF), F32),
            pltpu.VMEM((2, cells, HALF), F32),
            pltpu.VMEM((2, 56, HALF), F32),
            pltpu.VMEM((cells, HALF), F32),
            pltpu.VMEM((256, cells), BF16),
            pltpu.VMEM((256, cells), BF16),
            pltpu.VMEM((HID, cells), BF16),
            pltpu.VMEM((HID, cells), BF16),
            pltpu.VMEM((256, TT), F32),
            pltpu.VMEM((2, cells, HALF), F32),
            pltpu.VMEM((C, HB * HALF), F32),
            pltpu.VMEM((C, HB * HALF), F32),
        ],
        name="block",
    )(tile_pos, valid_rows, core_id, on_chip(mine), on_chip(theirs), inputs, stem_w, dw_kernel.T, norm_gain.reshape(1, C), w_in, w_out.T, cotangent[0])

    arrived = lax.ppermute(send, "lat", siblings)
    chip_sum = (own + arrived.astype(F32)).astype(BF16)
    every = [[i * lon + j for i in range(c, lat, 2) for j in range(lon)] for c in range(2)]
    part = lax.all_to_all(chip_sum, ("lat", "lon"), 0, 0, axis_index_groups=every, tiled=True)
    part = jnp.sum(part.astype(F32), axis=0)
    whole = part.astype(BF16)
    spread = jnp.broadcast_to(whole[None], (CHUNKS, 24, HALF))
    spread = lax.all_to_all(spread, ("lat", "lon"), 0, 0, axis_index_groups=every, tiled=True)
    other = lax.ppermute(spread, "lat", siblings)
    win, wout, ker, gain = pl.pallas_call(
        final_kernel,
        out_shape=(
            jax.ShapeDtypeStruct((C, HID), F32),
            jax.ShapeDtypeStruct((C, HID), F32),
            jax.ShapeDtypeStruct((KW * KW, C), F32),
            jax.ShapeDtypeStruct((1, C), F32),
        ),
        in_specs=[smem, vmem, vmem],
        out_specs=(vmem, vmem, vmem, vmem),
        scratch_shapes=[pltpu.VMEM((56, 256), F32)],
        name="finish",
    )(core_id, on_chip(spread), on_chip(other))
    return out_tiles[None], win, wout.T, ker.T, gain.reshape(C)


def solution(mesh):
    tiles = P("lon", "lat", None, None)
    in_specs = (tiles, P("lon", "lat"), P("lon", "lat"), P(), P(), P(), P(), P(), tiles)
    out_specs = (tiles, P(), P(), P(), P())
    return jax.shard_map(body, mesh=mesh, in_specs=in_specs, out_specs=out_specs, check_vma=False)
```

```python
import jax
import jax.numpy as jnp
import numpy as np
from jax import lax
from jax.experimental import pallas as pl
from jax.experimental.pallas import tpu as pltpu
from jax.sharding import PartitionSpec as P

C = 200
CIN = 77
HID = 800
KW = 7
TS = 16
TT = 256
A_DEV = 4
COLS = 8
TILE_ROWS = 64
HALF = 128
KPAD = 80
PIECE = 48
SHELL = 4 * PIECE
EDGE = A_DEV * PIECE
PAY = A_DEV * SHELL + 2 * EDGE
GROUP = 8
PITCH = 24
PROWS = TS + KW - 1
HB = 7
CHUNKS = 64
F32 = jnp.float32
BF16 = jnp.bfloat16
TN = (((0,), (0,)), ((), ()))
NT = (((1,), (1,)), ((), ()))
DIRS = [(dr, dc) for dr in (-1, 0, 1) for dc in (-1, 0, 1) if (dr, dc) != (0, 0)]


def shell_cells():
    m = np.arange(PIECE)
    left = (m // 3) * TS + m % 3
    pieces = np.concatenate([m, 13 * TS + m, left, left + 13, np.full(256 - SHELL, -1)])
    return pieces.reshape(1, 256).astype(np.int32)


def shell_kernel(pos_ref, rows_ref, x_ref, map_ref, shell_ref, east_ref, west_ref, kept_ref, flat, cut, buf):
    for k in range(CIN):
        for h in range(2):
            flat[h, A_DEV * k : A_DEV * k + A_DEV, :] = x_ref[k, :, h * HALF : (h + 1) * HALF].astype(F32)
    row = lax.broadcasted_iota(jnp.int32, (A_DEV * CIN, 1), 0) % A_DEV
    limit = jnp.full((A_DEV * CIN, 1), rows_ref[0, 0], jnp.int32)
    for a in range(1, A_DEV):
        limit = jnp.where(row == a, rows_ref[0, a], limit)
    cell_row = lax.broadcasted_iota(jnp.int32, (1, TT), 1) // TS
    for h in range(2):
        flat[h] = jnp.where(cell_row[:, h * HALF : (h + 1) * HALF] < limit, flat[h], 0.0)
    cell_id = lax.broadcasted_iota(jnp.int32, (TT, 256), 0)
    pick = (cell_id == map_ref[...]).astype(F32).astype(BF16)
    pieces = jnp.dot(flat[0].astype(BF16), pick[0:HALF], preferred_element_type=F32)
    pieces = pieces + jnp.dot(flat[1].astype(BF16), pick[HALF:TT], preferred_element_type=F32)
    cut[0] = pieces[:, 0:HALF]
    cut[1] = pieces[:, HALF:256]
    fill = lax.broadcasted_iota(jnp.int32, (3, 1), 0)
    buf[:, 768:1536] = jnp.zeros((KPAD, 768), F32)
    kept_ref[...] = jnp.zeros_like(kept_ref)
    for a in range(A_DEV):
        for h in range(2):
            kept_ref[a, 0:CIN, h * HALF : (h + 1) * HALF] = flat[h, pl.ds(a, CIN, stride=A_DEV), :].astype(BF16)
        v0 = cut[0, pl.ds(a, CIN, stride=A_DEV), :]
        v1 = cut[1, pl.ds(a, CIN, stride=A_DEV), :]
        place = pos_ref[0, a]
        tail = jnp.where(fill == 0, place // 16, jnp.where(fill == 1, place % 16, 0)).astype(F32)
        at = a * SHELL
        buf[0:CIN, at : at + HALF] = v0
        buf[0:CIN, at + HALF : at + SHELL] = v1[:, 0 : SHELL - HALF]
        buf[CIN:KPAD, at : at + SHELL] = jnp.broadcast_to(tail, (3, SHELL))
        east = 768 + a * PIECE
        west = 1152 + EDGE + a * PIECE
        buf[0:CIN, east : east + PIECE] = v1[:, 16:64]
        buf[CIN:KPAD, east : east + PIECE] = jnp.broadcast_to(tail, (3, PIECE))
        buf[0:CIN, west : west + 32] = v0[:, 96:HALF]
        buf[0:CIN, west + 32 : west + PIECE] = v1[:, 0:16]
        buf[CIN:KPAD, west : west + PIECE] = jnp.broadcast_to(tail, (3, PIECE))
    shell_ref[...] = buf[:, 0:768].astype(BF16)
    east_ref[...] = buf[:, 768:1152].astype(BF16)
    west_ref[...] = buf[:, 1152:1536].astype(BF16)


def gelu_parts(v):
    k = 0.7978845608028654
    sq = v * v
    u = 0.5 * jnp.tanh(v * (k + (k * 0.044715) * sq)) + 0.5
    value = v * u
    slope = u + (value - value * u) * (2.0 * k + (6.0 * k * 0.044715) * sq)
    return value, slope


def main_kernel(
    pos_ref, rows_ref, ga_ref, gb_ref, x_ref, sw_ref, dw_ref, gain_ref, wi_ref, wo_ref, cot_ref,
    out_ref, own_ref, send_ref,
    swp, dwt, gnp, wide, wit, wot, pm, tv, sm, ts, sem, lp, st, pt, cv, un, iv, ft, mg, hs, gps, gf, gc, si, so,
):
    swp[...] = jnp.zeros_like(swp)
    swp[0:CIN, 0:C] = sw_ref[...]
    dwt[1] = jnp.zeros((56, HALF), F32)
    dwt[0, 0 : KW * KW, :] = dw_ref[:, 0:HALF]
    dwt[1, 0 : KW * KW, 0 : C - HALF] = dw_ref[:, HALF:C]
    gnp[...] = jnp.zeros_like(gnp)
    gnp[:, 0:C] = gain_ref[...]
    gain0 = gnp[:, 0:HALF]
    gain1 = gnp[:, HALF:256]

    for g in range(GROUP):
        for j, ref in enumerate((ga_ref, gb_ref)):
            tail = ref[g, 64:KPAD, :].astype(F32)
            pm[2 * g + j : 2 * g + j + 1, :] = tail[13:14, :] * 16.0 + tail[14:15, :]
    lane = lax.broadcasted_iota(jnp.int32, (16, PAY), 1)
    slot = lax.broadcasted_iota(jnp.int32, (16, PAY), 0)
    kind = jnp.where(lane < 768, 0, jnp.where(lane < 768 + EDGE, 1, 2))
    first = jnp.where(lane < 768, lane % SHELL, (lane - 768) % PIECE) == 0
    label = jnp.where(first, pm[...] + 1000.0 * kind.astype(F32), -1.0)
    code = (slot * PAY + lane + 1).astype(F32)
    for a in range(A_DEV):
        q = pos_ref[0, a]
        row, col = q // COLS, q % COLS
        for n, (dr, dc) in enumerate(DIRS):
            nrow, ncol = row + dr, col + dc
            inside = (nrow >= 0) & (nrow < TILE_ROWS)
            side = jnp.where(ncol < 0, 1000, jnp.where(ncol >= COLS, 2000, 0))
            want = jnp.where(inside, nrow * COLS + (ncol + COLS) % COLS + side, -7)
            hit = jnp.where(label == want.astype(F32), code, 0.0)
            acc = jnp.sum(hit, axis=0, keepdims=True)
            folded = acc[:, 0:HALF]
            for i in range(1, PAY // HALF):
                folded = folded + acc[:, i * HALF : (i + 1) * HALF]
            tv[a * 8 + n : a * 8 + n + 1, :] = folded
    total = jnp.sum(tv[...], axis=1, keepdims=True)
    sm[...] = jnp.broadcast_to(total, (32, HALF)).astype(jnp.int32)
    tcopy = pltpu.make_async_copy(sm, ts, sem)
    tcopy.start()

    for a in range(A_DEV):
        rows = lax.dot_general(x_ref[a], swp[...], TN, preferred_element_type=F32)
        rows = rows.astype(BF16).astype(F32)
        for h in range(2):
            for y in range(TS):
                at = (a * PROWS + 3 + y) * PITCH + 3
                pt[h, at : at + TS, :] = rows[y * TS : (y + 1) * TS, h * HALF : (h + 1) * HALF]
    cell_row = lax.broadcasted_iota(jnp.int32, (1, TT), 1) // TS
    mg[...] = jnp.zeros_like(mg)
    for a in range(A_DEV):
        keep = cell_row < rows_ref[0, a]
        mg[0:C, a * TT : (a + 1) * TT] = jnp.where(keep, cot_ref[a].astype(F32), 0.0).astype(BF16)
    wide[C:256, :] = jnp.zeros((256 - C, HB * HALF), F32)
    wide[:, 768:896] = jnp.zeros((256, HALF), F32)
    for src, dst in ((wi_ref, wit), (wo_ref, wot)):
        wide[0:C, 0:HID] = src[...].astype(F32)
        for b in range(HB):
            dst[b * HALF : (b + 1) * HALF, :] = wide[:, b * HALF : (b + 1) * HALF].T.astype(BF16)
    tcopy.wait()

    gap = lax.broadcasted_iota(jnp.int32, (PIECE, 256), 1) - lax.broadcasted_iota(jnp.int32, (PIECE, 256), 0)
    for a in range(A_DEV):
        col = pos_ref[0, a] % COLS
        for n, (dr, dc) in enumerate(DIRS):
            got = ts[a * 8 + n, 0]
            if dc == 0:
                offset = 48 if dr < 0 else 0
            elif dc < 0:
                offset = jnp.where(col == 0, 0, 144)
            else:
                offset = jnp.where(col == COLS - 1, 0, 96)
            spot = jnp.maximum(got - 1, 0)
            source = spot // PAY
            at = spot - source * PAY + offset
            block = jnp.minimum(at // HALF, PAY // HALF - 2)
            shift = jnp.where(got == 0, -1000, at - block * HALF)
            cells = pl.ds(pl.multiple_of(block * HALF, HALF), 256)
            near = ga_ref[source // 2, :, cells]
            far = gb_ref[source // 2, :, cells]
            window = jnp.where(source % 2 == 0, near, far)
            pick = (gap == shift).astype(F32).astype(BF16)
            piece = lax.dot_general(pick, window, NT, preferred_element_type=F32)
            spot = (a * 8 + n) * PIECE
            lp[spot : spot + PIECE, 0:KPAD] = piece.astype(BF16)
    for a in range(A_DEV):
        span = slice(a * 8 * PIECE, (a + 1) * 8 * PIECE)
        rows = jnp.dot(lp[span, 0:KPAD], swp[...], preferred_element_type=F32)
        rows = rows.astype(BF16).astype(F32)
        st[0, span, :] = rows[:, 0:HALF]
        st[1, span, :] = rows[:, HALF:256]
    for a in range(A_DEV):
        base = {where: (a * 8 + n) * PIECE for n, where in enumerate(DIRS)}
        for h in range(2):
            for i in range(3):
                at = (a * PROWS + i) * PITCH
                low = at + 19 * PITCH
                up, down = base[-1, 0] + i * TS, base[1, 0] + i * TS
                pt[h, at + 3 : at + 3 + TS, :] = st[h, up : up + TS, :]
                pt[h, low + 3 : low + 3 + TS, :] = st[h, down : down + TS, :]
                for dc, xx in ((-1, 0), (1, 19)):
                    up, down = base[-1, dc] + 39 + 3 * i, base[1, dc] + 3 * i
                    pt[h, at + xx : at + xx + 3, :] = st[h, up : up + 3, :]
                    pt[h, low + xx : low + xx + 3, :] = st[h, down : down + 3, :]
            for y in range(TS):
                at = (a * PROWS + 3 + y) * PITCH
                for dc, xx in ((-1, 0), (1, 19)):
                    side = base[0, dc] + 3 * y
                    pt[h, at + xx : at + xx + 3, :] = st[h, side : side + 3, :]

    def conv_step(step, carry):
        h = step // (2 * A_DEV)
        part = step % (2 * A_DEV)
        at = pl.multiple_of((part // 2) * (PROWS * PITCH) + (part % 2) * (8 * PITCH), 8)
        acc = [jnp.zeros((TS, HALF), F32) for _ in range(8)]
        for r in range(KW):
            for k in range(KW):
                w = jnp.broadcast_to(dwt[h, r * KW + k : r * KW + k + 1, :], (TS, HALF))
                for y in range(8):
                    acc[y] = acc[y] + w * pt[h, pl.ds(at + (y + r) * PITCH + k, TS), :]
        for y in range(8):
            cv[h, pl.ds(pl.multiple_of(part * HALF, 8) + y * TS, TS), :] = acc[y]
        return carry

    lax.fori_loop(0, 4 * A_DEV, conv_step, 0)

    live = lax.broadcasted_iota(jnp.int32, (1, HALF), 1) < C - HALF
    for a in range(A_DEV):
        span = slice(a * TT, (a + 1) * TT)
        c0 = cv[0, span, :]
        c1 = cv[1, span, :]
        mean = jnp.sum(c0 + c1, axis=1, keepdims=True) * (1.0 / C)
        c0 = c0 - mean
        c1 = jnp.where(live, c1 - mean, 0.0)
        inv = lax.rsqrt(jnp.sum(c0 * c0 + c1 * c1, axis=1, keepdims=True) * (1.0 / C) + 1e-6)
        u0 = c0 * inv
        u1 = c1 * inv
        cv[0, span, :] = u0
        cv[1, span, :] = u1
        iv[span, :] = jnp.broadcast_to(inv, (TT, HALF))
        ft[0:HALF, span] = (u0 * gain0).T.astype(BF16)
        ft[HALF:256, span] = (u1 * gain1).T.astype(BF16)

    for b in range(HID // 80):
        span = slice(b * 80, (b + 1) * 80)
        preact = jnp.dot(wit[span, :], ft[...], preferred_element_type=F32)
        grad_hidden = jnp.dot(wot[span, :], mg[...], preferred_element_type=F32)
        value, slope = gelu_parts(preact)
        hs[span, :] = value.astype(BF16)
        gps[span, :] = (grad_hidden * slope).astype(BF16)
    gf[C:256, :] = jnp.zeros((256 - C, TT), F32)
    sums = [jnp.zeros((1, HALF), F32), jnp.zeros((1, HALF), F32)]
    for a in range(A_DEV):
        span = slice(a * TT, (a + 1) * TT)
        gf[0:C, :] = jnp.dot(wi_ref[...], gps[:, span], preferred_element_type=F32)
        g0 = gf[0:HALF, :].T.astype(BF16).astype(F32)
        g1 = gf[HALF:256, :].T.astype(BF16).astype(F32)
        u0 = cv[0, span, :]
        u1 = cv[1, span, :]
        inv = iv[span, :]
        sums[0] = sums[0] + jnp.sum(g0 * u0, axis=0, keepdims=True)
        sums[1] = sums[1] + jnp.sum(g1 * u1, axis=0, keepdims=True)
        d0 = g0 * gain0
        d1 = g1 * gain1
        m1 = jnp.sum(d0 + d1, axis=1, keepdims=True) * (1.0 / C)
        m2 = jnp.sum(d0 * u0 + d1 * u1, axis=1, keepdims=True) * (1.0 / C)
        gc[0, span, :] = inv * (d0 - m1 - u0 * m2)
        gc[1, span, :] = jnp.where(live, inv * (d1 - m1 - u1 * m2), 0.0)
        stem = lax.dot_general(swp[...], x_ref[a], TN, preferred_element_type=F32)[0:C, :].astype(BF16).astype(F32)
        branch = jnp.dot(wo_ref[...], hs[:, span], preferred_element_type=F32)
        keep = cell_row < rows_ref[0, a]
        out_ref[a] = jnp.where(keep, branch + stem, 0.0).astype(BF16)
    si[:, 768:896] = jnp.zeros((C, HALF), F32)
    so[:, 768:896] = jnp.zeros((C, HALF), F32)
    si[:, 0:HID] = lax.dot_general(ft[0:C, :], gps[...], NT, preferred_element_type=F32)
    so[:, 0:HID] = lax.dot_general(mg[0:C, :], hs[...], NT, preferred_element_type=F32)

    un[0, 48:56, :] = jnp.zeros((8, HALF), F32)
    un[1, 48:56, :] = jnp.zeros((8, HALF), F32)

    def tap_step(step, carry):
        h = step % 2
        r = step // 2
        down = pl.multiple_of(r * PITCH, 8)
        def tile_step(a, acc):
            acc = list(acc)
            at = pl.multiple_of(a * (PROWS * PITCH) + down, 8)
            for y in range(TS):
                g = gc[h, pl.ds(pl.multiple_of(a * TT, 8) + y * TS, TS), :]
                for k in range(KW):
                    acc[k] = acc[k] + g * pt[h, pl.ds(at + y * PITCH + k, TS), :]
            return tuple(acc)

        acc = lax.fori_loop(0, A_DEV, tile_step, tuple(jnp.zeros((TS, HALF), F32) for _ in range(KW)))
        for k in range(KW):
            un[h, pl.ds(r * KW + k, 1), :] = jnp.sum(acc[k], axis=0, keepdims=True)
        return carry

    lax.fori_loop(0, 2 * KW, tap_step, 0)
    un[0, 49:50, :] = sums[0]
    un[1, 49:50, :] = sums[1]

    lat_id = lax.axis_index("lat")
    is_low = lat_id % 2 == 0
    device = lat_id * lax.axis_size("lon") + lax.axis_index("lon")
    blank = jnp.zeros((8, HALF), F32)
    count = ((rows_ref[0, 0] + rows_ref[0, 1] + rows_ref[0, 2] + rows_ref[0, 3]) * TS).astype(F32)

    def blocks(t):
        if t < 25 * HB:
            r, b = t // HB, t % HB
            return si[8 * r : 8 * r + 8, b * HALF : (b + 1) * HALF], so[8 * r : 8 * r + 8, b * HALF : (b + 1) * HALF]
        t = t - 25 * HB
        if t < 14:
            return un[t // HB, 8 * (t % HB) : 8 * (t % HB) + 8, :], blank
        if t == 14:
            return jnp.where(lax.broadcasted_iota(jnp.int32, (8, HALF), 1) == device, count, blank), blank
        return blank, blank

    for chunk in range(CHUNKS):
        pairs = [blocks(3 * chunk + i) for i in range(3)]
        for i, (low, high) in enumerate(pairs):
            own_ref[chunk, 8 * i : 8 * i + 8, :] = jnp.where(is_low, low, high)
        sent = jnp.concatenate([jnp.where(is_low, high, low) for low, high in pairs], axis=0)
        send_ref[chunk] = sent.astype(BF16)


def final_kernel(own_ref, other_ref, win_ref, wout_ref, ker_ref, gain_ref, ks):
    is_low = lax.axis_index("lat") % 2 == 0

    def pair(chunk):
        own = own_ref[chunk].astype(F32)
        other = other_ref[chunk].astype(F32)
        return jnp.where(is_low, own, other), jnp.where(is_low, other, own)

    scale = 1.0 / jnp.sum(pair(CHUNKS - 1)[0][0:1, :], axis=1, keepdims=True)
    for chunk in range(CHUNKS - 1):
        low, high = pair(chunk)
        for i in range(3):
            t = 3 * chunk + i
            block = low[8 * i : 8 * i + 8, :] * scale
            if t < 25 * HB:
                r, b = t // HB, t % HB
                wide = HALF if b < HB - 1 else HID - (HB - 1) * HALF
                win_ref[8 * r : 8 * r + 8, b * HALF : b * HALF + wide] = block[:, 0:wide]
                turned = high[8 * i : 8 * i + 8, :] * scale
                wout_ref[8 * r : 8 * r + 8, b * HALF : b * HALF + wide] = turned[:, 0:wide]
            else:
                t = t - 25 * HB
                ks[8 * (t % HB) : 8 * (t % HB) + 8, (t // HB) * HALF : (t // HB + 1) * HALF] = block
    ker_ref[...] = ks[0 : KW * KW, 0:C]
    gain_ref[...] = ks[49:50, 0:C]


def on_chip(value):
    return pltpu.with_memory_space_constraint(value, pltpu.VMEM)


def body(x_tiles, tile_pos, valid_rows, stem_w, dw_kernel, norm_gain, w_in, w_out, cotangent):
    smem = pl.BlockSpec(memory_space=pltpu.SMEM)
    vmem = pl.BlockSpec(memory_space=pltpu.VMEM)
    shell, east, west, inputs = pl.pallas_call(
        shell_kernel,
        out_shape=(
            pltpu.VMEM((KPAD, 768), BF16),
            pltpu.VMEM((KPAD, 384), BF16),
            pltpu.VMEM((KPAD, 384), BF16),
            pltpu.VMEM((A_DEV, KPAD, TT), BF16),
        ),
        in_specs=[smem, smem, vmem, vmem],
        out_specs=(vmem, vmem, vmem, vmem),
        scratch_shapes=[
            pltpu.VMEM((2, A_DEV * CIN, HALF), F32),
            pltpu.VMEM((2, A_DEV * CIN, HALF), F32),
            pltpu.VMEM((KPAD, 1536), F32),
        ],
        compiler_params=pltpu.CompilerParams(vmem_limit_bytes=8 << 20),
        name="shell",
    )(tile_pos, valid_rows, x_tiles[0].transpose(1, 0, 2), jnp.asarray(shell_cells()))
    lon = lax.axis_size("lon")
    lat = lax.axis_size("lat")
    from_west = lax.ppermute(east, "lon", [(i, (i + 1) % lon) for i in range(lon)])
    from_east = lax.ppermute(west, "lon", [((i + 1) % lon, i) for i in range(lon)])
    payload = jnp.concatenate([shell, from_west + from_east], axis=1)
    same_core = [[i for i in range(c, lat, 2)] for c in range(2)]
    siblings = [(i, i ^ 1) for i in range(lat)]
    mine = lax.all_to_all(
        jnp.broadcast_to(payload[None], (GROUP, KPAD, PAY)), "lat", 0, 0, axis_index_groups=same_core, tiled=True
    )
    theirs = lax.ppermute(mine, "lat", siblings)

    cells = A_DEV * TT
    out_tiles, own, send = pl.pallas_call(
        main_kernel,
        out_shape=(
            jax.ShapeDtypeStruct((A_DEV, C, TT), BF16),
            pltpu.VMEM((CHUNKS, 24, HALF), F32),
            pltpu.VMEM((CHUNKS, 24, HALF), BF16),
        ),
        in_specs=[smem] * 2 + [vmem] * 9,
        out_specs=(vmem, vmem, vmem),
        scratch_shapes=[
            pltpu.VMEM((KPAD, 256), BF16),
            pltpu.VMEM((2, 56, HALF), F32),
            pltpu.VMEM((1, 256), F32),
            pltpu.VMEM((256, HB * HALF), F32),
            pltpu.VMEM((HB * HALF, 256), BF16),
            pltpu.VMEM((HB * HALF, 256), BF16),
            pltpu.VMEM((16, PAY), F32),
            pltpu.VMEM((32, HALF), F32),
            pltpu.VMEM((32, HALF), jnp.int32),
            pltpu.SMEM((32, HALF), jnp.int32),
            pltpu.SemaphoreType.DMA,
            pltpu.VMEM((32 * PIECE, HALF), BF16),
            pltpu.VMEM((2, 32 * PIECE, HALF), F32),
            pltpu.VMEM((2, A_DEV * PROWS * PITCH, HALF), F32),
            pltpu.VMEM((2, cells, HALF), F32),
            pltpu.VMEM((2, 56, HALF), F32),
            pltpu.VMEM((cells, HALF), F32),
            pltpu.VMEM((256, cells), BF16),
            pltpu.VMEM((256, cells), BF16),
            pltpu.VMEM((HID, cells), BF16),
            pltpu.VMEM((HID, cells), BF16),
            pltpu.VMEM((256, TT), F32),
            pltpu.VMEM((2, cells, HALF), F32),
            pltpu.VMEM((C, HB * HALF), F32),
            pltpu.VMEM((C, HB * HALF), F32),
        ],
        compiler_params=pltpu.CompilerParams(vmem_limit_bytes=32 << 20),
        name="block",
    )(tile_pos, valid_rows, on_chip(mine), on_chip(theirs), inputs, stem_w, dw_kernel.T, norm_gain.reshape(1, C), w_in, w_out.T, cotangent[0])

    arrived = lax.ppermute(send, "lat", siblings)
    chip_sum = (own + arrived.astype(F32)).astype(BF16)
    every = [[i * lon + j for i in range(c, lat, 2) for j in range(lon)] for c in range(2)]
    part = lax.all_to_all(chip_sum, ("lat", "lon"), 0, 0, axis_index_groups=every, tiled=True)
    part = jnp.sum(part.astype(F32), axis=0)
    whole = part.astype(BF16)
    spread = jnp.broadcast_to(whole[None], (CHUNKS, 24, HALF))
    spread = lax.all_to_all(spread, ("lat", "lon"), 0, 0, axis_index_groups=every, tiled=True)
    other = lax.ppermute(spread, "lat", siblings)
    win, wout, ker, gain = pl.pallas_call(
        final_kernel,
        out_shape=(
            jax.ShapeDtypeStruct((C, HID), F32),
            jax.ShapeDtypeStruct((C, HID), F32),
            jax.ShapeDtypeStruct((KW * KW, C), F32),
            jax.ShapeDtypeStruct((1, C), F32),
        ),
        in_specs=[vmem, vmem],
        out_specs=(vmem, vmem, vmem, vmem),
        scratch_shapes=[pltpu.VMEM((56, 256), F32)],
        compiler_params=pltpu.CompilerParams(vmem_limit_bytes=8 << 20),
        name="finish",
    )(on_chip(spread), on_chip(other))
    return out_tiles[None], win, wout.T, ker.T, gain.reshape(C)


def solution(mesh):
    tiles = P("lon", "lat", None, None)
    in_specs = (tiles, P("lon", "lat"), P("lon", "lat"), P(), P(), P(), P(), P(), tiles)
    out_specs = (tiles, P(), P(), P(), P())
    return jax.shard_map(body, mesh=mesh, in_specs=in_specs, out_specs=out_specs, check_vma=False)
```

```python
import jax
import jax.numpy as jnp
import numpy as np
from jax import lax
from jax.experimental import pallas as pl
from jax.experimental.pallas import tpu as pltpu
from jax.sharding import PartitionSpec as P

C = 200
CIN = 77
HID = 800
KW = 7
TS = 16
TT = 256
A_DEV = 4
COLS = 8
TILE_ROWS = 64
HALF = 128
KPAD = 80
PIECE = 48
SHELL = 160
PAY = A_DEV * SHELL
STRIP = 72
GROUP = 8
PITCH = 24
PROWS = TS + KW - 1
HB = 7
CHUNKS = 64
F32 = jnp.float32
BF16 = jnp.bfloat16
TN = (((0,), (0,)), ((), ()))
NT = (((1,), (1,)), ((), ()))
DIRS = [(dr, dc) for dr in (-1, 0, 1) for dc in (-1, 0, 1) if (dr, dc) != (0, 0)]


def shell_cells():
    m = np.arange(60)
    ends = (3 + m // 6) * TS + np.where(m % 6 < 3, m % 6, m % 6 + 10)
    cells = np.concatenate([np.arange(PIECE), 13 * TS + np.arange(PIECE), ends, np.full(100, -1)])
    return cells.reshape(1, 256).astype(np.int32)


def strip_sources():
    lane_of = {int(c): i for i, c in enumerate(shell_cells()[0]) if c >= 0}
    table = np.full((STRIP, HALF), -100000, np.int32)
    for j in range(3 * PROWS):
        row, c = j // 3 - 3, j % 3
        part = 0 if row < 0 else (1 if row < TS else 2)
        for side in range(2):
            table[j, 3 * side + part] = lane_of[(row % TS) * TS + (13 + c if side == 0 else c)]
    table[:PIECE, 6] = lane_of[13 * TS] + np.arange(PIECE)
    table[:PIECE, 7] = np.arange(PIECE)
    return table


def shell_kernel(pos_ref, rows_ref, x_ref, map_ref, shell_ref, kept_ref, flat, cut, buf):
    for k in range(CIN):
        for h in range(2):
            flat[h, A_DEV * k : A_DEV * k + A_DEV, :] = x_ref[k, :, h * HALF : (h + 1) * HALF].astype(F32)
    row = lax.broadcasted_iota(jnp.int32, (A_DEV * CIN, 1), 0) % A_DEV
    limit = jnp.full((A_DEV * CIN, 1), rows_ref[0, 0], jnp.int32)
    for a in range(1, A_DEV):
        limit = jnp.where(row == a, rows_ref[0, a], limit)
    cell_row = lax.broadcasted_iota(jnp.int32, (1, TT), 1) // TS
    for h in range(2):
        flat[h] = jnp.where(cell_row[:, h * HALF : (h + 1) * HALF] < limit, flat[h], 0.0)
    cell_id = lax.broadcasted_iota(jnp.int32, (TT, 256), 0)
    pick = (cell_id == map_ref[...]).astype(F32).astype(BF16)
    pieces = jnp.dot(flat[0].astype(BF16), pick[0:HALF], preferred_element_type=F32)
    pieces = pieces + jnp.dot(flat[1].astype(BF16), pick[HALF:TT], preferred_element_type=F32)
    cut[0] = pieces[:, 0:HALF]
    cut[1] = pieces[:, HALF:256]
    fill = lax.broadcasted_iota(jnp.int32, (3, 1), 0)
    kept_ref[...] = jnp.zeros_like(kept_ref)
    for a in range(A_DEV):
        for h in range(2):
            kept_ref[a, 0:CIN, h * HALF : (h + 1) * HALF] = flat[h, pl.ds(a, CIN, stride=A_DEV), :].astype(BF16)
        place = pos_ref[0, a]
        tail = jnp.where(fill == 0, place // 16, jnp.where(fill == 1, place % 16, 0)).astype(F32)
        at = a * SHELL
        buf[0:CIN, at : at + HALF] = cut[0, pl.ds(a, CIN, stride=A_DEV), :]
        buf[0:CIN, at + HALF : at + SHELL] = cut[1, pl.ds(a, CIN, stride=A_DEV), :][:, 0 : SHELL - HALF]
        buf[CIN:KPAD, at : at + SHELL] = jnp.broadcast_to(tail, (3, SHELL))
    shell_ref[...] = buf[...].astype(BF16)


def pick_kernel(
    pos_ref, east_ref, west_ref, ga_ref, gb_ref, src_ref,
    side_ref, band_ref, to_east_ref, to_west_ref,
    pm, tv, sm, ts, sem, gaps,
):
    for g in range(GROUP):
        for j, ref in enumerate((ga_ref, gb_ref)):
            tail = ref[g, 64:KPAD, :].astype(F32)
            pm[2 * g + j : 2 * g + j + 1, :] = tail[13:14, :] * 16.0 + tail[14:15, :]
    lane = lax.broadcasted_iota(jnp.int32, (16, PAY), 1)
    slot = lax.broadcasted_iota(jnp.int32, (16, PAY), 0)
    label = jnp.where(lane % SHELL == 0, pm[...], -1.0)
    code = (slot * 1024 + lane + 1).astype(F32)
    tv[...] = jnp.zeros_like(tv)

    def ask(entry, want):
        hit = jnp.where(label == want.astype(F32), code, 0.0)
        acc = jnp.sum(hit, axis=0, keepdims=True)
        folded = acc[:, 0:HALF]
        for i in range(1, PAY // HALF):
            folded = folded + acc[:, i * HALF : (i + 1) * HALF]
        tv[entry : entry + 1, :] = folded

    for a in range(A_DEV):
        q = pos_ref[0, a]
        row, col = q // COLS, q % COLS
        for n, (dr, dc) in enumerate(DIRS):
            nrow, ncol = row + dr, col + dc
            inside = (nrow >= 0) & (nrow < TILE_ROWS) & (ncol >= 0) & (ncol < COLS)
            ask(a * 8 + n, jnp.where(inside, nrow * COLS + ncol, -7))
        for first, ref, edge in ((32, east_ref, 0), (48, west_ref, COLS - 1)):
            q = ref[0, a]
            row, col = q // COLS, q % COLS
            for dr in (-1, 0, 1):
                inside = (row + dr >= 0) & (row + dr < TILE_ROWS) & (col == edge)
                ask(first + a * 4 + dr + 1, jnp.where(inside, (row + dr) * COLS + COLS - 1 - edge, -7))
    total = jnp.sum(tv[...], axis=1, keepdims=True)
    sm[...] = jnp.broadcast_to(total, (64, HALF)).astype(jnp.int32)
    tcopy = pltpu.make_async_copy(sm, ts, sem)
    tcopy.start()
    column = lax.broadcasted_iota(jnp.int32, (STRIP, 3 * HALF), 1)
    for n in range(8):
        gaps[n] = column - src_ref[:, n : n + 1]
    tcopy.wait()

    def take(entry, n, size):
        got = ts[entry, 0]
        spot = jnp.maximum(got - 1, 0)
        source = spot // 1024
        at = spot % 1024
        block = jnp.minimum(at // HALF, PAY // HALF - 3)
        shift = jnp.where(got == 0, -5000, at - block * HALF)
        cells = pl.ds(pl.multiple_of(block * HALF, HALF), 3 * HALF)
        near = ga_ref[source // 2, :, cells]
        far = gb_ref[source // 2, :, cells]
        window = jnp.where(source % 2 == 0, near, far)
        pick = (gaps[n, 0:size, :] == shift).astype(F32).astype(BF16)
        return lax.dot_general(pick, window, NT, preferred_element_type=F32)

    order = {where: n for n, where in enumerate(DIRS)}
    for a in range(A_DEV):
        rows = slice(a * STRIP, (a + 1) * STRIP)
        for side, dc in enumerate((-1, 1)):
            parts = [take(a * 8 + order[dr, dc], 3 * side + dr + 1, STRIP) for dr in (-1, 0, 1)]
            side_ref[side, rows, :] = (parts[0] + parts[1] + parts[2]).astype(BF16)
        band_ref[2 * a] = take(a * 8 + order[-1, 0], 6, PIECE).astype(BF16)
        band_ref[2 * a + 1] = take(a * 8 + order[1, 0], 7, PIECE).astype(BF16)
        for side, first, ref in ((0, 32, to_east_ref), (1, 48, to_west_ref)):
            parts = [take(first + a * 4 + dr + 1, 3 * side + dr + 1, STRIP) for dr in (-1, 0, 1)]
            ref[rows, :] = (parts[0] + parts[1] + parts[2]).astype(BF16)


def gelu_parts(v):
    k = 0.7978845608028654
    sq = v * v
    u = 0.5 * jnp.tanh(v * (k + (k * 0.044715) * sq)) + 0.5
    value = v * u
    slope = u + (value - value * u) * (2.0 * k + (6.0 * k * 0.044715) * sq)
    return value, slope


def main_kernel(
    rows_ref, side_ref, band_ref, west_ref, east_ref, x_ref, sw_ref, dw_ref, gain_ref, wi_ref, wo_ref, cot_ref,
    out_ref, own_ref, send_ref,
    swp, dwt, gnp, wide, wit, wot, pt, cv, un, iv, ft, mg, hs, gps, gf, gc, si, so,
):
    swp[...] = jnp.zeros_like(swp)
    swp[0:CIN, 0:C] = sw_ref[...]
    dwt[1] = jnp.zeros((56, HALF), F32)
    dwt[0, 0 : KW * KW, :] = dw_ref[:, 0:HALF]
    dwt[1, 0 : KW * KW, 0 : C - HALF] = dw_ref[:, HALF:C]
    gnp[...] = jnp.zeros_like(gnp)
    gnp[:, 0:C] = gain_ref[...]
    gain0 = gnp[:, 0:HALF]
    gain1 = gnp[:, HALF:256]

    for a in range(A_DEV):
        rows = lax.dot_general(x_ref[a], swp[...], TN, preferred_element_type=F32)
        rows = rows.astype(BF16).astype(F32)
        for h in range(2):
            for y in range(TS):
                at = (a * PROWS + 3 + y) * PITCH + 3
                pt[h, at : at + TS, :] = rows[y * TS : (y + 1) * TS, h * HALF : (h + 1) * HALF]
    cell_row = lax.broadcasted_iota(jnp.int32, (1, TT), 1) // TS
    mg[...] = jnp.zeros_like(mg)
    for a in range(A_DEV):
        keep = cell_row < rows_ref[0, a]
        mg[0:C, a * TT : (a + 1) * TT] = jnp.where(keep, cot_ref[a].astype(F32), 0.0).astype(BF16)
    wide[C:256, :] = jnp.zeros((256 - C, HB * HALF), F32)
    wide[:, 768:896] = jnp.zeros((256, HALF), F32)
    for src, dst in ((wi_ref, wit), (wo_ref, wot)):
        wide[0:C, 0:HID] = src[...].astype(F32)
        for b in range(HB):
            dst[b * HALF : (b + 1) * HALF, :] = wide[:, b * HALF : (b + 1) * HALF].T.astype(BF16)

    for side, (ref, xx) in enumerate(((west_ref, 0), (east_ref, 19))):
        cells = (side_ref[side].astype(F32) + ref[...].astype(F32)).astype(BF16)
        rows = jnp.dot(cells, swp[...], preferred_element_type=F32).astype(BF16).astype(F32)
        for h in range(2):
            for a in range(A_DEV):
                for y in range(PROWS):
                    at = (a * PROWS + y) * PITCH + xx
                    j = a * STRIP + 3 * y
                    pt[h, at : at + 3, :] = rows[j : j + 3, h * HALF : (h + 1) * HALF]
    for a in range(A_DEV):
        for n in range(2):
            rows = jnp.dot(band_ref[2 * a + n], swp[...], preferred_element_type=F32).astype(BF16).astype(F32)
            for h in range(2):
                for i in range(3):
                    at = (a * PROWS + 19 * n + i) * PITCH + 3
                    pt[h, at : at + TS, :] = rows[i * TS : (i + 1) * TS, h * HALF : (h + 1) * HALF]

    def conv_step(step, carry):
        h = step // (2 * A_DEV)
        part = step % (2 * A_DEV)
        at = pl.multiple_of((part // 2) * (PROWS * PITCH) + (part % 2) * (8 * PITCH), 8)
        acc = [jnp.zeros((TS, HALF), F32) for _ in range(8)]
        for r in range(KW):
            for k in range(KW):
                w = jnp.broadcast_to(dwt[h, r * KW + k : r * KW + k + 1, :], (TS, HALF))
                for y in range(8):
                    acc[y] = acc[y] + w * pt[h, pl.ds(at + (y + r) * PITCH + k, TS), :]
        for y in range(8):
            cv[h, pl.ds(pl.multiple_of(part * HALF, 8) + y * TS, TS), :] = acc[y]
        return carry

    lax.fori_loop(0, 4 * A_DEV, conv_step, 0)

    live = lax.broadcasted_iota(jnp.int32, (1, HALF), 1) < C - HALF
    for a in range(A_DEV):
        span = slice(a * TT, (a + 1) * TT)
        c0 = cv[0, span, :]
        c1 = cv[1, span, :]
        mean = jnp.sum(c0 + c1, axis=1, keepdims=True) * (1.0 / C)
        c0 = c0 - mean
        c1 = jnp.where(live, c1 - mean, 0.0)
        inv = lax.rsqrt(jnp.sum(c0 * c0 + c1 * c1, axis=1, keepdims=True) * (1.0 / C) + 1e-6)
        u0 = c0 * inv
        u1 = c1 * inv
        cv[0, span, :] = u0
        cv[1, span, :] = u1
        iv[span, :] = jnp.broadcast_to(inv, (TT, HALF))
        ft[0:HALF, span] = (u0 * gain0).T.astype(BF16)
        ft[HALF:256, span] = (u1 * gain1).T.astype(BF16)

    for b in range(HID // 80):
        span = slice(b * 80, (b + 1) * 80)
        preact = jnp.dot(wit[span, :], ft[...], preferred_element_type=F32)
        grad_hidden = jnp.dot(wot[span, :], mg[...], preferred_element_type=F32)
        value, slope = gelu_parts(preact)
        hs[span, :] = value.astype(BF16)
        gps[span, :] = (grad_hidden * slope).astype(BF16)
    gf[C:256, :] = jnp.zeros((256 - C, TT), F32)
    sums = [jnp.zeros((1, HALF), F32), jnp.zeros((1, HALF), F32)]
    for a in range(A_DEV):
        span = slice(a * TT, (a + 1) * TT)
        gf[0:C, :] = jnp.dot(wi_ref[...], gps[:, span], preferred_element_type=F32)
        g0 = gf[0:HALF, :].T.astype(BF16).astype(F32)
        g1 = gf[HALF:256, :].T.astype(BF16).astype(F32)
        u0 = cv[0, span, :]
        u1 = cv[1, span, :]
        inv = iv[span, :]
        sums[0] = sums[0] + jnp.sum(g0 * u0, axis=0, keepdims=True)
        sums[1] = sums[1] + jnp.sum(g1 * u1, axis=0, keepdims=True)
        d0 = g0 * gain0
        d1 = g1 * gain1
        m1 = jnp.sum(d0 + d1, axis=1, keepdims=True) * (1.0 / C)
        m2 = jnp.sum(d0 * u0 + d1 * u1, axis=1, keepdims=True) * (1.0 / C)
        gc[0, span, :] = inv * (d0 - m1 - u0 * m2)
        gc[1, span, :] = jnp.where(live, inv * (d1 - m1 - u1 * m2), 0.0)
        stem = lax.dot_general(swp[...], x_ref[a], TN, preferred_element_type=F32)[0:C, :].astype(BF16).astype(F32)
        branch = jnp.dot(wo_ref[...], hs[:, span], preferred_element_type=F32)
        keep = cell_row < rows_ref[0, a]
        out_ref[a] = jnp.where(keep, branch + stem, 0.0).astype(BF16)
    si[:, 768:896] = jnp.zeros((C, HALF), F32)
    so[:, 768:896] = jnp.zeros((C, HALF), F32)
    si[:, 0:HID] = lax.dot_general(ft[0:C, :], gps[...], NT, preferred_element_type=F32)
    so[:, 0:HID] = lax.dot_general(mg[0:C, :], hs[...], NT, preferred_element_type=F32)

    un[0, 48:56, :] = jnp.zeros((8, HALF), F32)
    un[1, 48:56, :] = jnp.zeros((8, HALF), F32)

    def tap_step(step, carry):
        h = step % 2
        r = step // 2
        down = pl.multiple_of(r * PITCH, 8)
        def tile_step(a, acc):
            acc = list(acc)
            at = pl.multiple_of(a * (PROWS * PITCH) + down, 8)
            for y in range(TS):
                g = gc[h, pl.ds(pl.multiple_of(a * TT, 8) + y * TS, TS), :]
                for k in range(KW):
                    acc[k] = acc[k] + g * pt[h, pl.ds(at + y * PITCH + k, TS), :]
            return tuple(acc)

        acc = lax.fori_loop(0, A_DEV, tile_step, tuple(jnp.zeros((TS, HALF), F32) for _ in range(KW)))
        for k in range(KW):
            un[h, pl.ds(r * KW + k, 1), :] = jnp.sum(acc[k], axis=0, keepdims=True)
        return carry

    lax.fori_loop(0, 2 * KW, tap_step, 0)
    un[0, 49:50, :] = sums[0]
    un[1, 49:50, :] = sums[1]

    lat_id = lax.axis_index("lat")
    is_low = lat_id % 2 == 0
    device = lat_id * lax.axis_size("lon") + lax.axis_index("lon")
    blank = jnp.zeros((8, HALF), F32)
    count = ((rows_ref[0, 0] + rows_ref[0, 1] + rows_ref[0, 2] + rows_ref[0, 3]) * TS).astype(F32)

    def blocks(t):
        if t < 25 * HB:
            r, b = t // HB, t % HB
            return si[8 * r : 8 * r + 8, b * HALF : (b + 1) * HALF], so[8 * r : 8 * r + 8, b * HALF : (b + 1) * HALF]
        t = t - 25 * HB
        if t < 14:
            return un[t // HB, 8 * (t % HB) : 8 * (t % HB) + 8, :], blank
        if t == 14:
            return jnp.where(lax.broadcasted_iota(jnp.int32, (8, HALF), 1) == device, count, blank), blank
        return blank, blank

    for chunk in range(CHUNKS):
        pairs = [blocks(3 * chunk + i) for i in range(3)]
        for i, (low, high) in enumerate(pairs):
            own_ref[chunk, 8 * i : 8 * i + 8, :] = jnp.where(is_low, low, high)
        sent = jnp.concatenate([jnp.where(is_low, high, low) for low, high in pairs], axis=0)
        send_ref[chunk] = sent.astype(BF16)


def final_kernel(own_ref, other_ref, win_ref, wout_ref, ker_ref, gain_ref, ks):
    is_low = lax.axis_index("lat") % 2 == 0

    def pair(chunk):
        own = own_ref[chunk].astype(F32)
        other = other_ref[chunk].astype(F32)
        return jnp.where(is_low, own, other), jnp.where(is_low, other, own)

    scale = 1.0 / jnp.sum(pair(CHUNKS - 1)[0][0:1, :], axis=1, keepdims=True)
    for chunk in range(CHUNKS - 1):
        low, high = pair(chunk)
        for i in range(3):
            t = 3 * chunk + i
            block = low[8 * i : 8 * i + 8, :] * scale
            if t < 25 * HB:
                r, b = t // HB, t % HB
                wide = HALF if b < HB - 1 else HID - (HB - 1) * HALF
                win_ref[8 * r : 8 * r + 8, b * HALF : b * HALF + wide] = block[:, 0:wide]
                turned = high[8 * i : 8 * i + 8, :] * scale
                wout_ref[8 * r : 8 * r + 8, b * HALF : b * HALF + wide] = turned[:, 0:wide]
            else:
                t = t - 25 * HB
                ks[8 * (t % HB) : 8 * (t % HB) + 8, (t // HB) * HALF : (t // HB + 1) * HALF] = block
    ker_ref[...] = ks[0 : KW * KW, 0:C]
    gain_ref[...] = ks[49:50, 0:C]


def on_chip(value):
    return pltpu.with_memory_space_constraint(value, pltpu.VMEM)


def body(x_tiles, tile_pos, valid_rows, stem_w, dw_kernel, norm_gain, w_in, w_out, cotangent):
    smem = pl.BlockSpec(memory_space=pltpu.SMEM)
    vmem = pl.BlockSpec(memory_space=pltpu.VMEM)
    lon = lax.axis_size("lon")
    lat = lax.axis_size("lat")
    eastward = [(i, (i + 1) % lon) for i in range(lon)]
    westward = [((i + 1) % lon, i) for i in range(lon)]
    pos_west = lax.ppermute(tile_pos, "lon", eastward)
    pos_east = lax.ppermute(tile_pos, "lon", westward)
    shell, inputs = pl.pallas_call(
        shell_kernel,
        out_shape=(pltpu.VMEM((KPAD, PAY), BF16), pltpu.VMEM((A_DEV, KPAD, TT), BF16)),
        in_specs=[smem, smem, vmem, vmem],
        out_specs=(vmem, vmem),
        scratch_shapes=[
            pltpu.VMEM((2, A_DEV * CIN, HALF), F32),
            pltpu.VMEM((2, A_DEV * CIN, HALF), F32),
            pltpu.VMEM((KPAD, PAY), F32),
        ],
        name="shell",
    )(tile_pos, valid_rows, x_tiles[0].transpose(1, 0, 2), jnp.asarray(shell_cells()))
    shell, pos_west, pos_east = lax.optimization_barrier((shell, pos_west, pos_east))
    same_core = [[i for i in range(c, lat, 2)] for c in range(2)]
    siblings = [(i, i ^ 1) for i in range(lat)]
    mine = lax.all_to_all(
        jnp.broadcast_to(shell[None], (GROUP, KPAD, PAY)), "lat", 0, 0, axis_index_groups=same_core, tiled=True
    )
    theirs = lax.ppermute(mine, "lat", siblings)
    side, band, to_east, to_west = pl.pallas_call(
        pick_kernel,
        out_shape=(
            pltpu.VMEM((2, A_DEV * STRIP, KPAD), BF16),
            pltpu.VMEM((2 * A_DEV, PIECE, KPAD), BF16),
            pltpu.VMEM((A_DEV * STRIP, KPAD), BF16),
            pltpu.VMEM((A_DEV * STRIP, KPAD), BF16),
        ),
        in_specs=[smem] * 3 + [vmem] * 3,
        out_specs=(vmem, vmem, vmem, vmem),
        scratch_shapes=[
            pltpu.VMEM((16, PAY), F32),
            pltpu.VMEM((64, HALF), F32),
            pltpu.VMEM((64, HALF), jnp.int32),
            pltpu.SMEM((64, HALF), jnp.int32),
            pltpu.SemaphoreType.DMA,
            pltpu.VMEM((8, STRIP, 3 * HALF), jnp.int32),
        ],
        compiler_params=pltpu.CompilerParams(vmem_limit_bytes=16 << 20),
        name="pick",
    )(tile_pos, pos_east, pos_west, on_chip(mine), on_chip(theirs), jnp.asarray(strip_sources()))
    from_west = lax.ppermute(to_east, "lon", eastward)
    from_east = lax.ppermute(to_west, "lon", westward)

    cells = A_DEV * TT
    out_tiles, own, send = pl.pallas_call(
        main_kernel,
        out_shape=(
            jax.ShapeDtypeStruct((A_DEV, C, TT), BF16),
            pltpu.VMEM((CHUNKS, 24, HALF), F32),
            pltpu.VMEM((CHUNKS, 24, HALF), BF16),
        ),
        in_specs=[smem] + [vmem] * 11,
        out_specs=(vmem, vmem, vmem),
        scratch_shapes=[
            pltpu.VMEM((KPAD, 256), BF16),
            pltpu.VMEM((2, 56, HALF), F32),
            pltpu.VMEM((1, 256), F32),
            pltpu.VMEM((256, HB * HALF), F32),
            pltpu.VMEM((HB * HALF, 256), BF16),
            pltpu.VMEM((HB * HALF, 256), BF16),
            pltpu.VMEM((2, A_DEV * PROWS * PITCH, HALF), F32),
            pltpu.VMEM((2, cells, HALF), F32),
            pltpu.VMEM((2, 56, HALF), F32),
            pltpu.VMEM((cells, HALF), F32),
            pltpu.VMEM((256, cells), BF16),
            pltpu.VMEM((256, cells), BF16),
            pltpu.VMEM((HID, cells), BF16),
            pltpu.VMEM((HID, cells), BF16),
            pltpu.VMEM((256, TT), F32),
            pltpu.VMEM((2, cells, HALF), F32),
            pltpu.VMEM((C, HB * HALF), F32),
            pltpu.VMEM((C, HB * HALF), F32),
        ],
        compiler_params=pltpu.CompilerParams(vmem_limit_bytes=32 << 20),
        name="block",
    )(valid_rows, side, band, on_chip(from_west), on_chip(from_east), inputs, stem_w, dw_kernel.T, norm_gain.reshape(1, C), w_in, w_out.T, cotangent[0])

    arrived = lax.ppermute(send, "lat", siblings)
    chip_sum = (own + arrived.astype(F32)).astype(BF16)
    every = [[i * lon + j for i in range(c, lat, 2) for j in range(lon)] for c in range(2)]
    part = lax.all_to_all(chip_sum, ("lat", "lon"), 0, 0, axis_index_groups=every, tiled=True)
    part = jnp.sum(part.astype(F32), axis=0)
    whole = part.astype(BF16)
    spread = jnp.broadcast_to(whole[None], (CHUNKS, 24, HALF))
    spread = lax.all_to_all(spread, ("lat", "lon"), 0, 0, axis_index_groups=every, tiled=True)
    other = lax.ppermute(spread, "lat", siblings)
    win, wout, ker, gain = pl.pallas_call(
        final_kernel,
        out_shape=(
            jax.ShapeDtypeStruct((C, HID), F32),
            jax.ShapeDtypeStruct((C, HID), F32),
            jax.ShapeDtypeStruct((KW * KW, C), F32),
            jax.ShapeDtypeStruct((1, C), F32),
        ),
        in_specs=[vmem, vmem],
        out_specs=(vmem, vmem, vmem, vmem),
        scratch_shapes=[pltpu.VMEM((56, 256), F32)],
        compiler_params=pltpu.CompilerParams(vmem_limit_bytes=8 << 20),
        name="finish",
    )(on_chip(spread), on_chip(other))
    return out_tiles[None], win, wout.T, ker.T, gain.reshape(C)


def solution(mesh):
    tiles = P("lon", "lat", None, None)
    in_specs = (tiles, P("lon", "lat"), P("lon", "lat"), P(), P(), P(), P(), P(), tiles)
    out_specs = (tiles, P(), P(), P(), P())
    return jax.shard_map(body, mesh=mesh, in_specs=in_specs, out_specs=out_specs, check_vma=False)
```

```python
import jax
import jax.numpy as jnp
import numpy as np
from jax import lax
from jax.experimental import pallas as pl
from jax.experimental.pallas import tpu as pltpu
from jax.sharding import PartitionSpec as P

C = 200
CIN = 77
HID = 800
KW = 7
TS = 16
TT = 256
A_DEV = 4
COLS = 8
TILE_ROWS = 64
HALF = 128
KPAD = 80
PIECE = 48
SHELL = 160
PAY = A_DEV * SHELL
STRIP = 72
GROUP = 8
PITCH = 24
PROWS = TS + KW - 1
HB = 7
CHUNKS = 64
F32 = jnp.float32
BF16 = jnp.bfloat16
TN = (((0,), (0,)), ((), ()))
NT = (((1,), (1,)), ((), ()))
DIRS = [(dr, dc) for dr in (-1, 0, 1) for dc in (-1, 0, 1) if (dr, dc) != (0, 0)]


def shell_cells():
    m = np.arange(60)
    ends = (3 + m // 6) * TS + np.where(m % 6 < 3, m % 6, m % 6 + 10)
    cells = np.concatenate([np.arange(PIECE), 13 * TS + np.arange(PIECE), ends, np.full(100, -1)])
    return cells.reshape(1, 256).astype(np.int32)


def strip_sources():
    lane_of = {int(c): i for i, c in enumerate(shell_cells()[0]) if c >= 0}
    table = np.full((STRIP, HALF), -100000, np.int32)
    for j in range(3 * PROWS):
        row, c = j // 3 - 3, j % 3
        part = 0 if row < 0 else (1 if row < TS else 2)
        for side in range(2):
            table[j, 3 * side + part] = lane_of[(row % TS) * TS + (13 + c if side == 0 else c)]
    table[:PIECE, 6] = lane_of[13 * TS] + np.arange(PIECE)
    table[:PIECE, 7] = np.arange(PIECE)
    return table


def shell_kernel(pos_ref, rows_ref, x_ref, map_ref, shell_ref, kept_ref, flat, cut, buf):
    for k in range(CIN):
        for h in range(2):
            flat[h, A_DEV * k : A_DEV * k + A_DEV, :] = x_ref[k, :, h * HALF : (h + 1) * HALF].astype(F32)
    row = lax.broadcasted_iota(jnp.int32, (A_DEV * CIN, 1), 0) % A_DEV
    limit = jnp.full((A_DEV * CIN, 1), rows_ref[0, 0], jnp.int32)
    for a in range(1, A_DEV):
        limit = jnp.where(row == a, rows_ref[0, a], limit)
    cell_row = lax.broadcasted_iota(jnp.int32, (1, TT), 1) // TS
    for h in range(2):
        flat[h] = jnp.where(cell_row[:, h * HALF : (h + 1) * HALF] < limit, flat[h], 0.0)
    cell_id = lax.broadcasted_iota(jnp.int32, (TT, 256), 0)
    pick = (cell_id == map_ref[...]).astype(F32).astype(BF16)
    pieces = jnp.dot(flat[0].astype(BF16), pick[0:HALF], preferred_element_type=F32)
    pieces = pieces + jnp.dot(flat[1].astype(BF16), pick[HALF:TT], preferred_element_type=F32)
    cut[0] = pieces[:, 0:HALF]
    cut[1] = pieces[:, HALF:256]
    fill = lax.broadcasted_iota(jnp.int32, (3, 1), 0)
    kept_ref[...] = jnp.zeros_like(kept_ref)
    for a in range(A_DEV):
        for h in range(2):
            kept_ref[a, 0:CIN, h * HALF : (h + 1) * HALF] = flat[h, pl.ds(a, CIN, stride=A_DEV), :].astype(BF16)
        place = pos_ref[0, a]
        tail = jnp.where(fill == 0, place // 16, jnp.where(fill == 1, place % 16, 0)).astype(F32)
        at = a * SHELL
        buf[0:CIN, at : at + HALF] = cut[0, pl.ds(a, CIN, stride=A_DEV), :]
        buf[0:CIN, at + HALF : at + SHELL] = cut[1, pl.ds(a, CIN, stride=A_DEV), :][:, 0 : SHELL - HALF]
        buf[CIN:KPAD, at : at + SHELL] = jnp.broadcast_to(tail, (3, SHELL))
    shell_ref[...] = buf[...].astype(BF16)


def pick_kernel(
    pos_ref, first_pos_ref, second_pos_ref, ga_ref, gb_ref, src_ref,
    side_ref, band_ref, first_ref, second_ref,
    pm, tv, sm, ts, sem, gaps,
):
    for g in range(GROUP):
        for j, ref in enumerate((ga_ref, gb_ref)):
            tail = ref[g, 64:KPAD, :].astype(F32)
            pm[2 * g + j : 2 * g + j + 1, :] = tail[13:14, :] * 16.0 + tail[14:15, :]
    lane = lax.broadcasted_iota(jnp.int32, (16, PAY), 1)
    slot = lax.broadcasted_iota(jnp.int32, (16, PAY), 0)
    label = jnp.where(lane % SHELL == 0, pm[...], -1.0)
    code = (slot * 1024 + lane + 1).astype(F32)
    tv[...] = jnp.zeros_like(tv)
    odd = lax.axis_index("lon") % 2
    near_edge = odd * (COLS - 1)

    def ask(entry, want):
        hit = jnp.where(label == want.astype(F32), code, 0.0)
        acc = jnp.sum(hit, axis=0, keepdims=True)
        folded = acc[:, 0:HALF]
        for i in range(1, PAY // HALF):
            folded = folded + acc[:, i * HALF : (i + 1) * HALF]
        tv[entry : entry + 1, :] = folded

    for a in range(A_DEV):
        q = pos_ref[0, a]
        row, col = q // COLS, q % COLS
        for n, (dr, dc) in enumerate(DIRS):
            nrow, ncol = row + dr, col + dc
            inside = (nrow >= 0) & (nrow < TILE_ROWS) & (ncol >= 0) & (ncol < COLS)
            ask(a * 8 + n, jnp.where(inside, nrow * COLS + ncol, -7))
        for first, ref, edge in ((32, first_pos_ref, near_edge), (48, second_pos_ref, COLS - 1 - near_edge)):
            q = ref[0, a]
            row, col = q // COLS, q % COLS
            for dr in (-1, 0, 1):
                inside = (row + dr >= 0) & (row + dr < TILE_ROWS) & (col == edge)
                ask(first + a * 4 + dr + 1, jnp.where(inside, (row + dr) * COLS + COLS - 1 - edge, -7))
    total = jnp.sum(tv[...], axis=1, keepdims=True)
    sm[...] = jnp.broadcast_to(total, (64, HALF)).astype(jnp.int32)
    tcopy = pltpu.make_async_copy(sm, ts, sem)
    tcopy.start()
    column = lax.broadcasted_iota(jnp.int32, (STRIP, 3 * HALF), 1)
    for n in range(8):
        gaps[n] = column - src_ref[:, n : n + 1]
    tcopy.wait()

    def take(entry, n, size):
        got = ts[entry, 0]
        spot = jnp.maximum(got - 1, 0)
        source = spot // 1024
        at = spot % 1024
        block = jnp.minimum(at // HALF, PAY // HALF - 3)
        shift = jnp.where(got == 0, -5000, at - block * HALF)
        cells = pl.ds(pl.multiple_of(block * HALF, HALF), 3 * HALF)
        near = ga_ref[source // 2, :, cells]
        far = gb_ref[source // 2, :, cells]
        window = jnp.where(source % 2 == 0, near, far)
        pick = (gaps[n, 0:size, :] == shift).astype(F32).astype(BF16)
        return lax.dot_general(pick, window, NT, preferred_element_type=F32)

    order = {where: n for n, where in enumerate(DIRS)}
    for a in range(A_DEV):
        rows = slice(a * STRIP, (a + 1) * STRIP)
        for side, dc in enumerate((-1, 1)):
            parts = [take(a * 8 + order[dr, dc], 3 * side + dr + 1, STRIP) for dr in (-1, 0, 1)]
            side_ref[side, rows, :] = (parts[0] + parts[1] + parts[2]).astype(BF16)
        band_ref[2 * a] = take(a * 8 + order[-1, 0], 6, PIECE).astype(BF16)
        band_ref[2 * a + 1] = take(a * 8 + order[1, 0], 7, PIECE).astype(BF16)
        for side, first, ref in ((odd, 32, first_ref), (1 - odd, 48, second_ref)):
            parts = [take(first + a * 4 + dr + 1, 3 * side + dr + 1, STRIP) for dr in (-1, 0, 1)]
            ref[rows, :] = (parts[0] + parts[1] + parts[2]).astype(BF16)


def gelu_parts(v):
    k = 0.7978845608028654
    sq = v * v
    u = 0.5 * jnp.tanh(v * (k + (k * 0.044715) * sq)) + 0.5
    value = v * u
    slope = u + (value - value * u) * (2.0 * k + (6.0 * k * 0.044715) * sq)
    return value, slope


def main_kernel(
    rows_ref, side_ref, band_ref, first_ref, second_ref, x_ref, sw_ref, dw_ref, gain_ref, wi_ref, wo_ref, cot_ref,
    out_ref, own_ref, send_ref,
    swp, dwt, gnp, wide, wit, wot, pt, cv, un, iv, ft, mg, hs, gps, gf, gc, si, so,
):
    swp[...] = jnp.zeros_like(swp)
    swp[0:CIN, 0:C] = sw_ref[...]
    dwt[1] = jnp.zeros((56, HALF), F32)
    dwt[0, 0 : KW * KW, :] = dw_ref[:, 0:HALF]
    dwt[1, 0 : KW * KW, 0 : C - HALF] = dw_ref[:, HALF:C]
    gnp[...] = jnp.zeros_like(gnp)
    gnp[:, 0:C] = gain_ref[...]
    gain0 = gnp[:, 0:HALF]
    gain1 = gnp[:, HALF:256]

    for a in range(A_DEV):
        rows = lax.dot_general(x_ref[a], swp[...], TN, preferred_element_type=F32)
        rows = rows.astype(BF16).astype(F32)
        for h in range(2):
            for y in range(TS):
                at = (a * PROWS + 3 + y) * PITCH + 3
                pt[h, at : at + TS, :] = rows[y * TS : (y + 1) * TS, h * HALF : (h + 1) * HALF]
    cell_row = lax.broadcasted_iota(jnp.int32, (1, TT), 1) // TS
    mg[...] = jnp.zeros_like(mg)
    for a in range(A_DEV):
        keep = cell_row < rows_ref[0, a]
        mg[0:C, a * TT : (a + 1) * TT] = jnp.where(keep, cot_ref[a].astype(F32), 0.0).astype(BF16)
    wide[C:256, :] = jnp.zeros((256 - C, HB * HALF), F32)
    wide[:, 768:896] = jnp.zeros((256, HALF), F32)
    for src, dst in ((wi_ref, wit), (wo_ref, wot)):
        wide[0:C, 0:HID] = src[...].astype(F32)
        for b in range(HB):
            dst[b * HALF : (b + 1) * HALF, :] = wide[:, b * HALF : (b + 1) * HALF].T.astype(BF16)

    odd = lax.axis_index("lon") % 2 == 1
    for side, (even_ref, odd_ref, xx) in enumerate(((second_ref, first_ref, 0), (first_ref, second_ref, 19))):
        arrived = jnp.where(odd, odd_ref[...].astype(F32), even_ref[...].astype(F32))
        cells = (side_ref[side].astype(F32) + arrived).astype(BF16)
        rows = jnp.dot(cells, swp[...], preferred_element_type=F32).astype(BF16).astype(F32)
        for h in range(2):
            for a in range(A_DEV):
                for y in range(PROWS):
                    at = (a * PROWS + y) * PITCH + xx
                    j = a * STRIP + 3 * y
                    pt[h, at : at + 3, :] = rows[j : j + 3, h * HALF : (h + 1) * HALF]
    for a in range(A_DEV):
        for n in range(2):
            rows = jnp.dot(band_ref[2 * a + n], swp[...], preferred_element_type=F32).astype(BF16).astype(F32)
            for h in range(2):
                for i in range(3):
                    at = (a * PROWS + 19 * n + i) * PITCH + 3
                    pt[h, at : at + TS, :] = rows[i * TS : (i + 1) * TS, h * HALF : (h + 1) * HALF]

    def conv_step(step, carry):
        h = step // (2 * A_DEV)
        part = step % (2 * A_DEV)
        at = pl.multiple_of((part // 2) * (PROWS * PITCH) + (part % 2) * (8 * PITCH), 8)
        acc = [jnp.zeros((TS, HALF), F32) for _ in range(8)]
        for r in range(KW):
            for k in range(KW):
                w = jnp.broadcast_to(dwt[h, r * KW + k : r * KW + k + 1, :], (TS, HALF))
                for y in range(8):
                    acc[y] = acc[y] + w * pt[h, pl.ds(at + (y + r) * PITCH + k, TS), :]
        for y in range(8):
            cv[h, pl.ds(pl.multiple_of(part * HALF, 8) + y * TS, TS), :] = acc[y]
        return carry

    lax.fori_loop(0, 4 * A_DEV, conv_step, 0)

    live = lax.broadcasted_iota(jnp.int32, (1, HALF), 1) < C - HALF
    for a in range(A_DEV):
        span = slice(a * TT, (a + 1) * TT)
        c0 = cv[0, span, :]
        c1 = cv[1, span, :]
        mean = jnp.sum(c0 + c1, axis=1, keepdims=True) * (1.0 / C)
        c0 = c0 - mean
        c1 = jnp.where(live, c1 - mean, 0.0)
        inv = lax.rsqrt(jnp.sum(c0 * c0 + c1 * c1, axis=1, keepdims=True) * (1.0 / C) + 1e-6)
        u0 = c0 * inv
        u1 = c1 * inv
        cv[0, span, :] = u0
        cv[1, span, :] = u1
        iv[span, :] = jnp.broadcast_to(inv, (TT, HALF))
        ft[0:HALF, span] = (u0 * gain0).T.astype(BF16)
        ft[HALF:256, span] = (u1 * gain1).T.astype(BF16)

    for b in range(HID // 80):
        span = slice(b * 80, (b + 1) * 80)
        preact = jnp.dot(wit[span, :], ft[...], preferred_element_type=F32)
        grad_hidden = jnp.dot(wot[span, :], mg[...], preferred_element_type=F32)
        value, slope = gelu_parts(preact)
        hs[span, :] = value.astype(BF16)
        gps[span, :] = (grad_hidden * slope).astype(BF16)
    gf[C:256, :] = jnp.zeros((256 - C, TT), F32)
    sums = [jnp.zeros((1, HALF), F32), jnp.zeros((1, HALF), F32)]
    for a in range(A_DEV):
        span = slice(a * TT, (a + 1) * TT)
        gf[0:C, :] = jnp.dot(wi_ref[...], gps[:, span], preferred_element_type=F32)
        g0 = gf[0:HALF, :].T.astype(BF16).astype(F32)
        g1 = gf[HALF:256, :].T.astype(BF16).astype(F32)
        u0 = cv[0, span, :]
        u1 = cv[1, span, :]
        inv = iv[span, :]
        sums[0] = sums[0] + jnp.sum(g0 * u0, axis=0, keepdims=True)
        sums[1] = sums[1] + jnp.sum(g1 * u1, axis=0, keepdims=True)
        d0 = g0 * gain0
        d1 = g1 * gain1
        m1 = jnp.sum(d0 + d1, axis=1, keepdims=True) * (1.0 / C)
        m2 = jnp.sum(d0 * u0 + d1 * u1, axis=1, keepdims=True) * (1.0 / C)
        gc[0, span, :] = inv * (d0 - m1 - u0 * m2)
        gc[1, span, :] = jnp.where(live, inv * (d1 - m1 - u1 * m2), 0.0)
        stem = lax.dot_general(swp[...], x_ref[a], TN, preferred_element_type=F32)[0:C, :].astype(BF16).astype(F32)
        branch = jnp.dot(wo_ref[...], hs[:, span], preferred_element_type=F32)
        keep = cell_row < rows_ref[0, a]
        out_ref[a] = jnp.where(keep, branch + stem, 0.0).astype(BF16)
    si[:, 768:896] = jnp.zeros((C, HALF), F32)
    so[:, 768:896] = jnp.zeros((C, HALF), F32)
    si[:, 0:HID] = lax.dot_general(ft[0:C, :], gps[...], NT, preferred_element_type=F32)
    so[:, 0:HID] = lax.dot_general(mg[0:C, :], hs[...], NT, preferred_element_type=F32)

    un[0, 48:56, :] = jnp.zeros((8, HALF), F32)
    un[1, 48:56, :] = jnp.zeros((8, HALF), F32)

    def tap_step(step, carry):
        h = step % 2
        r = step // 2
        down = pl.multiple_of(r * PITCH, 8)
        def tile_step(a, acc):
            acc = list(acc)
            at = pl.multiple_of(a * (PROWS * PITCH) + down, 8)
            for y in range(TS):
                g = gc[h, pl.ds(pl.multiple_of(a * TT, 8) + y * TS, TS), :]
                for k in range(KW):
                    acc[k] = acc[k] + g * pt[h, pl.ds(at + y * PITCH + k, TS), :]
            return tuple(acc)

        acc = lax.fori_loop(0, A_DEV, tile_step, tuple(jnp.zeros((TS, HALF), F32) for _ in range(KW)))
        for k in range(KW):
            un[h, pl.ds(r * KW + k, 1), :] = jnp.sum(acc[k], axis=0, keepdims=True)
        return carry

    lax.fori_loop(0, 2 * KW, tap_step, 0)
    un[0, 49:50, :] = sums[0]
    un[1, 49:50, :] = sums[1]

    lat_id = lax.axis_index("lat")
    is_low = lat_id % 2 == 0
    device = lat_id * lax.axis_size("lon") + lax.axis_index("lon")
    blank = jnp.zeros((8, HALF), F32)
    count = ((rows_ref[0, 0] + rows_ref[0, 1] + rows_ref[0, 2] + rows_ref[0, 3]) * TS).astype(F32)

    def blocks(t):
        if t < 25 * HB:
            r, b = t // HB, t % HB
            return si[8 * r : 8 * r + 8, b * HALF : (b + 1) * HALF], so[8 * r : 8 * r + 8, b * HALF : (b + 1) * HALF]
        t = t - 25 * HB
        if t < 14:
            return un[t // HB, 8 * (t % HB) : 8 * (t % HB) + 8, :], blank
        if t == 14:
            return jnp.where(lax.broadcasted_iota(jnp.int32, (8, HALF), 1) == device, count, blank), blank
        return blank, blank

    for chunk in range(CHUNKS):
        pairs = [blocks(3 * chunk + i) for i in range(3)]
        for i, (low, high) in enumerate(pairs):
            own_ref[chunk, 8 * i : 8 * i + 8, :] = jnp.where(is_low, low, high)
        sent = jnp.concatenate([jnp.where(is_low, high, low) for low, high in pairs], axis=0)
        send_ref[chunk] = sent.astype(BF16)


def final_kernel(own_ref, other_ref, win_ref, wout_ref, ker_ref, gain_ref, ks):
    is_low = lax.axis_index("lat") % 2 == 0

    def pair(chunk):
        own = own_ref[chunk].astype(F32)
        other = other_ref[chunk].astype(F32)
        return jnp.where(is_low, own, other), jnp.where(is_low, other, own)

    scale = 1.0 / jnp.sum(pair(CHUNKS - 1)[0][0:1, :], axis=1, keepdims=True)
    for chunk in range(CHUNKS - 1):
        low, high = pair(chunk)
        for i in range(3):
            t = 3 * chunk + i
            block = low[8 * i : 8 * i + 8, :] * scale
            if t < 25 * HB:
                r, b = t // HB, t % HB
                wide = HALF if b < HB - 1 else HID - (HB - 1) * HALF
                win_ref[8 * r : 8 * r + 8, b * HALF : b * HALF + wide] = block[:, 0:wide]
                turned = high[8 * i : 8 * i + 8, :] * scale
                wout_ref[8 * r : 8 * r + 8, b * HALF : b * HALF + wide] = turned[:, 0:wide]
            else:
                t = t - 25 * HB
                ks[8 * (t % HB) : 8 * (t % HB) + 8, (t // HB) * HALF : (t // HB + 1) * HALF] = block
    ker_ref[...] = ks[0 : KW * KW, 0:C]
    gain_ref[...] = ks[49:50, 0:C]


def on_chip(value):
    return pltpu.with_memory_space_constraint(value, pltpu.VMEM)


def in_hbm(value):
    return pltpu.with_memory_space_constraint(value, pltpu.HBM)


def body(x_tiles, tile_pos, valid_rows, stem_w, dw_kernel, norm_gain, w_in, w_out, cotangent):
    smem = pl.BlockSpec(memory_space=pltpu.SMEM)
    vmem = pl.BlockSpec(memory_space=pltpu.VMEM)
    lon = lax.axis_size("lon")
    lat = lax.axis_size("lat")
    first_pair = [(i, i ^ 1) for i in range(lon)]
    second_pair = [(i, (i + 1 if i % 2 else i - 1) % lon) for i in range(lon)]
    pos_second = lax.ppermute(tile_pos, "lon", second_pair)
    pos_first = lax.ppermute(tile_pos, "lon", first_pair)
    shell, inputs = pl.pallas_call(
        shell_kernel,
        out_shape=(pltpu.VMEM((KPAD, PAY), BF16), pltpu.VMEM((A_DEV, KPAD, TT), BF16)),
        in_specs=[smem, smem, vmem, vmem],
        out_specs=(vmem, vmem),
        scratch_shapes=[
            pltpu.VMEM((2, A_DEV * CIN, HALF), F32),
            pltpu.VMEM((2, A_DEV * CIN, HALF), F32),
            pltpu.VMEM((KPAD, PAY), F32),
        ],
        name="shell",
    )(tile_pos, valid_rows, x_tiles[0].transpose(1, 0, 2), jnp.asarray(shell_cells()))
    shell, pos_first, pos_second = lax.optimization_barrier((shell, pos_first, pos_second))
    same_core = [[i for i in range(c, lat, 2)] for c in range(2)]
    siblings = [(i, i ^ 1) for i in range(lat)]
    mine = lax.all_to_all(
        jnp.broadcast_to(shell[None], (GROUP, KPAD, PAY)), "lat", 0, 0, axis_index_groups=same_core, tiled=True
    )
    theirs = lax.ppermute(mine, "lat", siblings)
    side, band, to_first, to_second = pl.pallas_call(
        pick_kernel,
        out_shape=(
            pltpu.VMEM((2, A_DEV * STRIP, KPAD), BF16),
            pltpu.VMEM((2 * A_DEV, PIECE, KPAD), BF16),
            pltpu.VMEM((A_DEV * STRIP, KPAD), BF16),
            pltpu.VMEM((A_DEV * STRIP, KPAD), BF16),
        ),
        in_specs=[smem] * 3 + [vmem] * 3,
        out_specs=(vmem, vmem, vmem, vmem),
        scratch_shapes=[
            pltpu.VMEM((16, PAY), F32),
            pltpu.VMEM((64, HALF), F32),
            pltpu.VMEM((64, HALF), jnp.int32),
            pltpu.SMEM((64, HALF), jnp.int32),
            pltpu.SemaphoreType.DMA,
            pltpu.VMEM((8, STRIP, 3 * HALF), jnp.int32),
        ],
        compiler_params=pltpu.CompilerParams(vmem_limit_bytes=16 << 20),
        name="pick",
    )(tile_pos, pos_first, pos_second, on_chip(mine), on_chip(theirs), jnp.asarray(strip_sources()))
    from_second = lax.ppermute(to_second, "lon", second_pair)
    from_first = lax.ppermute(to_first, "lon", first_pair)

    cells = A_DEV * TT
    out_tiles, own, send = pl.pallas_call(
        main_kernel,
        out_shape=(
            jax.ShapeDtypeStruct((A_DEV, C, TT), BF16),
            pltpu.VMEM((CHUNKS, 24, HALF), F32),
            pltpu.VMEM((CHUNKS, 24, HALF), BF16),
        ),
        in_specs=[smem] + [vmem] * 11,
        out_specs=(vmem, vmem, vmem),
        scratch_shapes=[
            pltpu.VMEM((KPAD, 256), BF16),
            pltpu.VMEM((2, 56, HALF), F32),
            pltpu.VMEM((1, 256), F32),
            pltpu.VMEM((256, HB * HALF), F32),
            pltpu.VMEM((HB * HALF, 256), BF16),
            pltpu.VMEM((HB * HALF, 256), BF16),
            pltpu.VMEM((2, A_DEV * PROWS * PITCH, HALF), F32),
            pltpu.VMEM((2, cells, HALF), F32),
            pltpu.VMEM((2, 56, HALF), F32),
            pltpu.VMEM((cells, HALF), F32),
            pltpu.VMEM((256, cells), BF16),
            pltpu.VMEM((256, cells), BF16),
            pltpu.VMEM((HID, cells), BF16),
            pltpu.VMEM((HID, cells), BF16),
            pltpu.VMEM((256, TT), F32),
            pltpu.VMEM((2, cells, HALF), F32),
            pltpu.VMEM((C, HB * HALF), F32),
            pltpu.VMEM((C, HB * HALF), F32),
        ],
        compiler_params=pltpu.CompilerParams(vmem_limit_bytes=32 << 20),
        name="block",
    )(in_hbm(valid_rows), side, band, on_chip(from_first), on_chip(from_second), inputs, stem_w, dw_kernel.T, norm_gain.reshape(1, C), w_in, w_out.T, cotangent[0])

    arrived = lax.ppermute(send, "lat", siblings)
    chip_sum = (own + arrived.astype(F32)).astype(BF16)
    every = [[i * lon + j for i in range(c, lat, 2) for j in range(lon)] for c in range(2)]
    part = lax.all_to_all(chip_sum, ("lat", "lon"), 0, 0, axis_index_groups=every, tiled=True)
    part = jnp.sum(part.astype(F32), axis=0)
    whole = part.astype(BF16)
    spread = jnp.broadcast_to(whole[None], (CHUNKS, 24, HALF))
    spread = lax.all_to_all(spread, ("lat", "lon"), 0, 0, axis_index_groups=every, tiled=True)
    other = lax.ppermute(spread, "lat", siblings)
    win, wout, ker, gain = pl.pallas_call(
        final_kernel,
        out_shape=(
            jax.ShapeDtypeStruct((C, HID), F32),
            jax.ShapeDtypeStruct((C, HID), F32),
            jax.ShapeDtypeStruct((KW * KW, C), F32),
            jax.ShapeDtypeStruct((1, C), F32),
        ),
        in_specs=[vmem, vmem],
        out_specs=(vmem, vmem, vmem, vmem),
        scratch_shapes=[pltpu.VMEM((56, 256), F32)],
        compiler_params=pltpu.CompilerParams(vmem_limit_bytes=8 << 20),
        name="finish",
    )(on_chip(spread), on_chip(other))
    return out_tiles[None], win, wout.T, ker.T, gain.reshape(C)


def solution(mesh):
    tiles = P("lon", "lat", None, None)
    in_specs = (tiles, P("lon", "lat"), P("lon", "lat"), P(), P(), P(), P(), P(), tiles)
    out_specs = (tiles, P(), P(), P(), P())
    return jax.shard_map(body, mesh=mesh, in_specs=in_specs, out_specs=out_specs, check_vma=False)
```

```python
import jax
import jax.numpy as jnp
import numpy as np
from jax import lax
from jax.experimental import pallas as pl
from jax.experimental.pallas import tpu as pltpu
from jax.sharding import PartitionSpec as P

C = 200
CIN = 77
HID = 800
KW = 7
TS = 16
TT = 256
A_DEV = 4
COLS = 8
TILE_ROWS = 64
HALF = 128
KPAD = 80
PIECE = 48
SHELL = 160
PAY = A_DEV * SHELL
STRIP = 72
GROUP = 8
PITCH = 24
PROWS = TS + KW - 1
HB = 7
CHUNKS = 64
F32 = jnp.float32
BF16 = jnp.bfloat16
TN = (((0,), (0,)), ((), ()))
NT = (((1,), (1,)), ((), ()))
DIRS = [(dr, dc) for dr in (-1, 0, 1) for dc in (-1, 0, 1) if (dr, dc) != (0, 0)]


def shell_cells():
    m = np.arange(60)
    ends = (3 + m // 6) * TS + np.where(m % 6 < 3, m % 6, m % 6 + 10)
    cells = np.concatenate([np.arange(PIECE), 13 * TS + np.arange(PIECE), ends, np.full(100, -1)])
    return cells.reshape(1, 256).astype(np.int32)


def strip_sources():
    lane_of = {int(c): i for i, c in enumerate(shell_cells()[0]) if c >= 0}
    table = np.full((STRIP, HALF), -100000, np.int32)
    for j in range(3 * PROWS):
        row, c = j // 3 - 3, j % 3
        part = 0 if row < 0 else (1 if row < TS else 2)
        for side in range(2):
            table[j, 3 * side + part] = lane_of[(row % TS) * TS + (13 + c if side == 0 else c)]
    table[:PIECE, 6] = lane_of[13 * TS] + np.arange(PIECE)
    table[:PIECE, 7] = np.arange(PIECE)
    return table


def shell_kernel(pos_ref, rows_ref, x_ref, map_ref, shell_ref, kept_ref, flat, cut, buf):
    for k in range(CIN):
        for h in range(2):
            flat[h, A_DEV * k : A_DEV * k + A_DEV, :] = x_ref[k, :, h * HALF : (h + 1) * HALF].astype(F32)
    row = lax.broadcasted_iota(jnp.int32, (A_DEV * CIN, 1), 0) % A_DEV
    limit = jnp.full((A_DEV * CIN, 1), rows_ref[0, 0], jnp.int32)
    for a in range(1, A_DEV):
        limit = jnp.where(row == a, rows_ref[0, a], limit)
    cell_row = lax.broadcasted_iota(jnp.int32, (1, TT), 1) // TS
    for h in range(2):
        flat[h] = jnp.where(cell_row[:, h * HALF : (h + 1) * HALF] < limit, flat[h], 0.0)
    cell_id = lax.broadcasted_iota(jnp.int32, (TT, 256), 0)
    pick = (cell_id == map_ref[...]).astype(F32).astype(BF16)
    pieces = jnp.dot(flat[0].astype(BF16), pick[0:HALF], preferred_element_type=F32)
    pieces = pieces + jnp.dot(flat[1].astype(BF16), pick[HALF:TT], preferred_element_type=F32)
    cut[0] = pieces[:, 0:HALF]
    cut[1] = pieces[:, HALF:256]
    fill = lax.broadcasted_iota(jnp.int32, (3, 1), 0)
    kept_ref[...] = jnp.zeros_like(kept_ref)
    for a in range(A_DEV):
        for h in range(2):
            kept_ref[a, 0:CIN, h * HALF : (h + 1) * HALF] = flat[h, pl.ds(a, CIN, stride=A_DEV), :].astype(BF16)
        place = pos_ref[0, a]
        tail = jnp.where(fill == 0, place // 16, jnp.where(fill == 1, place % 16, 0)).astype(F32)
        at = a * SHELL
        buf[0:CIN, at : at + HALF] = cut[0, pl.ds(a, CIN, stride=A_DEV), :]
        buf[0:CIN, at + HALF : at + SHELL] = cut[1, pl.ds(a, CIN, stride=A_DEV), :][:, 0 : SHELL - HALF]
        buf[CIN:KPAD, at : at + SHELL] = jnp.broadcast_to(tail, (3, SHELL))
    shell_ref[...] = buf[...].astype(BF16)


def pick_kernel(
    pos_ref, far_pos_ref, ga_ref, gb_ref, src_ref,
    side_ref, band_ref, give_ref,
    pm, tv, sm, ts, sem, gaps,
):
    for g in range(GROUP):
        for j, ref in enumerate((ga_ref, gb_ref)):
            tail = ref[g, 64:KPAD, :].astype(F32)
            pm[2 * g + j : 2 * g + j + 1, :] = tail[13:14, :] * 16.0 + tail[14:15, :]
    lane = lax.broadcasted_iota(jnp.int32, (16, PAY), 1)
    slot = lax.broadcasted_iota(jnp.int32, (16, PAY), 0)
    label = jnp.where(lane % SHELL == 0, pm[...], -1.0)
    code = (slot * 1024 + lane + 1).astype(F32)
    tv[...] = jnp.zeros_like(tv)
    odd = lax.axis_index("lat") % 2
    near_edge = odd * (COLS - 1)

    def ask(entry, want):
        hit = jnp.where(label == want.astype(F32), code, 0.0)
        acc = jnp.sum(hit, axis=0, keepdims=True)
        folded = acc[:, 0:HALF]
        for i in range(1, PAY // HALF):
            folded = folded + acc[:, i * HALF : (i + 1) * HALF]
        tv[entry : entry + 1, :] = folded

    for a in range(A_DEV):
        q = pos_ref[0, a]
        row, col = q // COLS, q % COLS
        for n, (dr, dc) in enumerate(DIRS):
            nrow, ncol = row + dr, col + dc
            inside = (nrow >= 0) & (nrow < TILE_ROWS) & (ncol >= 0) & (ncol < COLS)
            ask(a * 8 + n, jnp.where(inside, nrow * COLS + ncol, -7))
        for first, i in ((32, 0), (48, 1)):
            q = far_pos_ref[i, a]
            row, col = q // COLS, q % COLS
            for dr in (-1, 0, 1):
                inside = (row + dr >= 0) & (row + dr < TILE_ROWS) & (col == near_edge)
                ask(first + a * 4 + dr + 1, jnp.where(inside, (row + dr) * COLS + COLS - 1 - near_edge, -7))
    total = jnp.sum(tv[...], axis=1, keepdims=True)
    sm[...] = jnp.broadcast_to(total, (64, HALF)).astype(jnp.int32)
    tcopy = pltpu.make_async_copy(sm, ts, sem)
    tcopy.start()
    column = lax.broadcasted_iota(jnp.int32, (STRIP, 3 * HALF), 1)
    for n in range(8):
        gaps[n] = column - src_ref[:, n : n + 1]
    tcopy.wait()

    def take(entry, n, size):
        got = ts[entry, 0]
        spot = jnp.maximum(got - 1, 0)
        source = spot // 1024
        at = spot % 1024
        block = jnp.minimum(at // HALF, PAY // HALF - 3)
        shift = jnp.where(got == 0, -5000, at - block * HALF)
        cells = pl.ds(pl.multiple_of(block * HALF, HALF), 3 * HALF)
        near = ga_ref[source // 2, :, cells]
        far = gb_ref[source // 2, :, cells]
        window = jnp.where(source % 2 == 0, near, far)
        pick = (gaps[n, 0:size, :] == shift).astype(F32).astype(BF16)
        return lax.dot_general(pick, window, NT, preferred_element_type=F32)

    order = {where: n for n, where in enumerate(DIRS)}
    for a in range(A_DEV):
        rows = slice(a * STRIP, (a + 1) * STRIP)
        for side, dc in enumerate((-1, 1)):
            parts = [take(a * 8 + order[dr, dc], 3 * side + dr + 1, STRIP) for dr in (-1, 0, 1)]
            side_ref[side, rows, :] = (parts[0] + parts[1] + parts[2]).astype(BF16)
        band_ref[2 * a] = take(a * 8 + order[-1, 0], 6, PIECE).astype(BF16)
        band_ref[2 * a + 1] = take(a * 8 + order[1, 0], 7, PIECE).astype(BF16)
        for i, first in ((0, 32), (1, 48)):
            parts = [take(first + a * 4 + dr + 1, 3 * odd + dr + 1, STRIP) for dr in (-1, 0, 1)]
            give_ref[i, rows, :] = (parts[0] + parts[1] + parts[2]).astype(BF16)


def gelu_parts(v):
    k = 0.7978845608028654
    sq = v * v
    u = 0.5 * jnp.tanh(v * (k + (k * 0.044715) * sq)) + 0.5
    value = v * u
    slope = u + (value - value * u) * (2.0 * k + (6.0 * k * 0.044715) * sq)
    return value, slope


def main_kernel(
    rows_ref, side_ref, band_ref, near_ref, swap_ref, x_ref, sw_ref, dw_ref, gain_ref, wi_ref, wo_ref, cot_ref,
    out_ref, own_ref, send_ref,
    swp, dwt, gnp, wide, wit, wot, pt, cv, un, iv, ft, mg, hs, gps, gf, gc, si, so,
):
    swp[...] = jnp.zeros_like(swp)
    swp[0:CIN, 0:C] = sw_ref[...]
    dwt[1] = jnp.zeros((56, HALF), F32)
    dwt[0, 0 : KW * KW, :] = dw_ref[:, 0:HALF]
    dwt[1, 0 : KW * KW, 0 : C - HALF] = dw_ref[:, HALF:C]
    gnp[...] = jnp.zeros_like(gnp)
    gnp[:, 0:C] = gain_ref[...]
    gain0 = gnp[:, 0:HALF]
    gain1 = gnp[:, HALF:256]

    for a in range(A_DEV):
        rows = lax.dot_general(x_ref[a], swp[...], TN, preferred_element_type=F32)
        rows = rows.astype(BF16).astype(F32)
        for h in range(2):
            for y in range(TS):
                at = (a * PROWS + 3 + y) * PITCH + 3
                pt[h, at : at + TS, :] = rows[y * TS : (y + 1) * TS, h * HALF : (h + 1) * HALF]
    cell_row = lax.broadcasted_iota(jnp.int32, (1, TT), 1) // TS
    mg[...] = jnp.zeros_like(mg)
    for a in range(A_DEV):
        keep = cell_row < rows_ref[0, a]
        mg[0:C, a * TT : (a + 1) * TT] = jnp.where(keep, cot_ref[a].astype(F32), 0.0).astype(BF16)
    wide[C:256, :] = jnp.zeros((256 - C, HB * HALF), F32)
    wide[:, 768:896] = jnp.zeros((256, HALF), F32)
    for src, dst in ((wi_ref, wit), (wo_ref, wot)):
        wide[0:C, 0:HID] = src[...].astype(F32)
        for b in range(HB):
            dst[b * HALF : (b + 1) * HALF, :] = wide[:, b * HALF : (b + 1) * HALF].T.astype(BF16)

    odd = lax.axis_index("lat") % 2 == 1
    near = near_ref[0].astype(F32)
    swap = swap_ref[1].astype(F32)
    for side, (even, other, xx) in enumerate(((near, swap, 0), (swap, near, 19))):
        arrived = jnp.where(odd, other, even)
        cells = (side_ref[side].astype(F32) + arrived).astype(BF16)
        rows = jnp.dot(cells, swp[...], preferred_element_type=F32).astype(BF16).astype(F32)
        for h in range(2):
            for a in range(A_DEV):
                for y in range(PROWS):
                    at = (a * PROWS + y) * PITCH + xx
                    j = a * STRIP + 3 * y
                    pt[h, at : at + 3, :] = rows[j : j + 3, h * HALF : (h + 1) * HALF]
    for a in range(A_DEV):
        for n in range(2):
            rows = jnp.dot(band_ref[2 * a + n], swp[...], preferred_element_type=F32).astype(BF16).astype(F32)
            for h in range(2):
                for i in range(3):
                    at = (a * PROWS + 19 * n + i) * PITCH + 3
                    pt[h, at : at + TS, :] = rows[i * TS : (i + 1) * TS, h * HALF : (h + 1) * HALF]

    def conv_step(step, carry):
        h = step // (2 * A_DEV)
        part = step % (2 * A_DEV)
        at = pl.multiple_of((part // 2) * (PROWS * PITCH) + (part % 2) * (8 * PITCH), 8)
        acc = [jnp.zeros((TS, HALF), F32) for _ in range(8)]
        for r in range(KW):
            for k in range(KW):
                w = jnp.broadcast_to(dwt[h, r * KW + k : r * KW + k + 1, :], (TS, HALF))
                for y in range(8):
                    acc[y] = acc[y] + w * pt[h, pl.ds(at + (y + r) * PITCH + k, TS), :]
        for y in range(8):
            cv[h, pl.ds(pl.multiple_of(part * HALF, 8) + y * TS, TS), :] = acc[y]
        return carry

    lax.fori_loop(0, 4 * A_DEV, conv_step, 0)

    live = lax.broadcasted_iota(jnp.int32, (1, HALF), 1) < C - HALF
    for a in range(A_DEV):
        span = slice(a * TT, (a + 1) * TT)
        c0 = cv[0, span, :]
        c1 = cv[1, span, :]
        mean = jnp.sum(c0 + c1, axis=1, keepdims=True) * (1.0 / C)
        c0 = c0 - mean
        c1 = jnp.where(live, c1 - mean, 0.0)
        inv = lax.rsqrt(jnp.sum(c0 * c0 + c1 * c1, axis=1, keepdims=True) * (1.0 / C) + 1e-6)
        u0 = c0 * inv
        u1 = c1 * inv
        cv[0, span, :] = u0
        cv[1, span, :] = u1
        iv[span, :] = jnp.broadcast_to(inv, (TT, HALF))
        ft[0:HALF, span] = (u0 * gain0).T.astype(BF16)
        ft[HALF:256, span] = (u1 * gain1).T.astype(BF16)

    for b in range(HID // 80):
        span = slice(b * 80, (b + 1) * 80)
        preact = jnp.dot(wit[span, :], ft[...], preferred_element_type=F32)
        grad_hidden = jnp.dot(wot[span, :], mg[...], preferred_element_type=F32)
        value, slope = gelu_parts(preact)
        hs[span, :] = value.astype(BF16)
        gps[span, :] = (grad_hidden * slope).astype(BF16)
    gf[C:256, :] = jnp.zeros((256 - C, TT), F32)
    sums = [jnp.zeros((1, HALF), F32), jnp.zeros((1, HALF), F32)]
    for a in range(A_DEV):
        span = slice(a * TT, (a + 1) * TT)
        gf[0:C, :] = jnp.dot(wi_ref[...], gps[:, span], preferred_element_type=F32)
        g0 = gf[0:HALF, :].T.astype(BF16).astype(F32)
        g1 = gf[HALF:256, :].T.astype(BF16).astype(F32)
        u0 = cv[0, span, :]
        u1 = cv[1, span, :]
        inv = iv[span, :]
        sums[0] = sums[0] + jnp.sum(g0 * u0, axis=0, keepdims=True)
        sums[1] = sums[1] + jnp.sum(g1 * u1, axis=0, keepdims=True)
        d0 = g0 * gain0
        d1 = g1 * gain1
        m1 = jnp.sum(d0 + d1, axis=1, keepdims=True) * (1.0 / C)
        m2 = jnp.sum(d0 * u0 + d1 * u1, axis=1, keepdims=True) * (1.0 / C)
        gc[0, span, :] = inv * (d0 - m1 - u0 * m2)
        gc[1, span, :] = jnp.where(live, inv * (d1 - m1 - u1 * m2), 0.0)
        stem = lax.dot_general(swp[...], x_ref[a], TN, preferred_element_type=F32)[0:C, :].astype(BF16).astype(F32)
        branch = jnp.dot(wo_ref[...], hs[:, span], preferred_element_type=F32)
        keep = cell_row < rows_ref[0, a]
        out_ref[a] = jnp.where(keep, branch + stem, 0.0).astype(BF16)
    si[:, 768:896] = jnp.zeros((C, HALF), F32)
    so[:, 768:896] = jnp.zeros((C, HALF), F32)
    si[:, 0:HID] = lax.dot_general(ft[0:C, :], gps[...], NT, preferred_element_type=F32)
    so[:, 0:HID] = lax.dot_general(mg[0:C, :], hs[...], NT, preferred_element_type=F32)

    un[0, 48:56, :] = jnp.zeros((8, HALF), F32)
    un[1, 48:56, :] = jnp.zeros((8, HALF), F32)

    def tap_step(step, carry):
        h = step % 2
        r = step // 2
        down = pl.multiple_of(r * PITCH, 8)
        def tile_step(a, acc):
            acc = list(acc)
            at = pl.multiple_of(a * (PROWS * PITCH) + down, 8)
            for y in range(TS):
                g = gc[h, pl.ds(pl.multiple_of(a * TT, 8) + y * TS, TS), :]
                for k in range(KW):
                    acc[k] = acc[k] + g * pt[h, pl.ds(at + y * PITCH + k, TS), :]
            return tuple(acc)

        acc = lax.fori_loop(0, A_DEV, tile_step, tuple(jnp.zeros((TS, HALF), F32) for _ in range(KW)))
        for k in range(KW):
            un[h, pl.ds(r * KW + k, 1), :] = jnp.sum(acc[k], axis=0, keepdims=True)
        return carry

    lax.fori_loop(0, 2 * KW, tap_step, 0)
    un[0, 49:50, :] = sums[0]
    un[1, 49:50, :] = sums[1]

    lat_id = lax.axis_index("lat")
    is_low = lat_id % 2 == 0
    device = lat_id * lax.axis_size("lon") + lax.axis_index("lon")
    blank = jnp.zeros((8, HALF), F32)
    count = ((rows_ref[0, 0] + rows_ref[0, 1] + rows_ref[0, 2] + rows_ref[0, 3]) * TS).astype(F32)

    def blocks(t):
        if t < 25 * HB:
            r, b = t // HB, t % HB
            return si[8 * r : 8 * r + 8, b * HALF : (b + 1) * HALF], so[8 * r : 8 * r + 8, b * HALF : (b + 1) * HALF]
        t = t - 25 * HB
        if t < 14:
            return un[t // HB, 8 * (t % HB) : 8 * (t % HB) + 8, :], blank
        if t == 14:
            return jnp.where(lax.broadcasted_iota(jnp.int32, (8, HALF), 1) == device, count, blank), blank
        return blank, blank

    for chunk in range(CHUNKS):
        pairs = [blocks(3 * chunk + i) for i in range(3)]
        for i, (low, high) in enumerate(pairs):
            own_ref[chunk, 8 * i : 8 * i + 8, :] = jnp.where(is_low, low, high)
        sent = jnp.concatenate([jnp.where(is_low, high, low) for low, high in pairs], axis=0)
        send_ref[chunk] = sent.astype(BF16)


def final_kernel(own_ref, other_ref, win_ref, wout_ref, ker_ref, gain_ref, ks):
    is_low = lax.axis_index("lat") % 2 == 0

    def pair(chunk):
        own = own_ref[chunk].astype(F32)
        other = other_ref[chunk].astype(F32)
        return jnp.where(is_low, own, other), jnp.where(is_low, other, own)

    scale = 1.0 / jnp.sum(pair(CHUNKS - 1)[0][0:1, :], axis=1, keepdims=True)
    for chunk in range(CHUNKS - 1):
        low, high = pair(chunk)
        for i in range(3):
            t = 3 * chunk + i
            block = low[8 * i : 8 * i + 8, :] * scale
            if t < 25 * HB:
                r, b = t // HB, t % HB
                wide = HALF if b < HB - 1 else HID - (HB - 1) * HALF
                win_ref[8 * r : 8 * r + 8, b * HALF : b * HALF + wide] = block[:, 0:wide]
                turned = high[8 * i : 8 * i + 8, :] * scale
                wout_ref[8 * r : 8 * r + 8, b * HALF : b * HALF + wide] = turned[:, 0:wide]
            else:
                t = t - 25 * HB
                ks[8 * (t % HB) : 8 * (t % HB) + 8, (t // HB) * HALF : (t // HB + 1) * HALF] = block
    ker_ref[...] = ks[0 : KW * KW, 0:C]
    gain_ref[...] = ks[49:50, 0:C]


def on_chip(value):
    return pltpu.with_memory_space_constraint(value, pltpu.VMEM)


def in_hbm(value):
    return pltpu.with_memory_space_constraint(value, pltpu.HBM)


def body(x_tiles, tile_pos, valid_rows, stem_w, dw_kernel, norm_gain, w_in, w_out, cotangent):
    smem = pl.BlockSpec(memory_space=pltpu.SMEM)
    vmem = pl.BlockSpec(memory_space=pltpu.VMEM)
    lon = lax.axis_size("lon")
    lat = lax.axis_size("lat")
    hop = [(i * lon + j, i * lon + (j + (1 if i % 2 == 0 else -1)) % lon) for i in range(lat) for j in range(lon)]
    back = [(target, source) for source, target in hop]
    siblings = [(i, i ^ 1) for i in range(lat)]
    pos_pair = jnp.concatenate([tile_pos, lax.ppermute(tile_pos, "lat", siblings)], axis=0)
    pos_far = lax.ppermute(pos_pair, ("lat", "lon"), back)
    shell, inputs = pl.pallas_call(
        shell_kernel,
        out_shape=(pltpu.VMEM((KPAD, PAY), BF16), pltpu.VMEM((A_DEV, KPAD, TT), BF16)),
        in_specs=[smem, smem, vmem, vmem],
        out_specs=(vmem, vmem),
        scratch_shapes=[
            pltpu.VMEM((2, A_DEV * CIN, HALF), F32),
            pltpu.VMEM((2, A_DEV * CIN, HALF), F32),
            pltpu.VMEM((KPAD, PAY), F32),
        ],
        name="shell",
    )(tile_pos, valid_rows, x_tiles[0].transpose(1, 0, 2), jnp.asarray(shell_cells()))
    shell, pos_far = lax.optimization_barrier((shell, pos_far))
    same_core = [[i for i in range(c, lat, 2)] for c in range(2)]
    mine = lax.all_to_all(
        jnp.broadcast_to(shell[None], (GROUP, KPAD, PAY)), "lat", 0, 0, axis_index_groups=same_core, tiled=True
    )
    theirs = lax.ppermute(mine, "lat", siblings)
    side, band, give = pl.pallas_call(
        pick_kernel,
        out_shape=(
            pltpu.VMEM((2, A_DEV * STRIP, KPAD), BF16),
            pltpu.VMEM((2 * A_DEV, PIECE, KPAD), BF16),
            pltpu.VMEM((2, A_DEV * STRIP, KPAD), BF16),
        ),
        in_specs=[smem] * 2 + [vmem] * 3,
        out_specs=(vmem, vmem, vmem),
        scratch_shapes=[
            pltpu.VMEM((16, PAY), F32),
            pltpu.VMEM((64, HALF), F32),
            pltpu.VMEM((64, HALF), jnp.int32),
            pltpu.SMEM((64, HALF), jnp.int32),
            pltpu.SemaphoreType.DMA,
            pltpu.VMEM((8, STRIP, 3 * HALF), jnp.int32),
        ],
        compiler_params=pltpu.CompilerParams(vmem_limit_bytes=16 << 20),
        name="pick",
    )(tile_pos, pos_far, on_chip(mine), on_chip(theirs), jnp.asarray(strip_sources()))
    near = lax.ppermute(give, ("lat", "lon"), hop)
    swap = lax.ppermute(near, "lat", siblings)

    cells = A_DEV * TT
    out_tiles, own, send = pl.pallas_call(
        main_kernel,
        out_shape=(
            jax.ShapeDtypeStruct((A_DEV, C, TT), BF16),
            pltpu.VMEM((CHUNKS, 24, HALF), F32),
            pltpu.VMEM((CHUNKS, 24, HALF), BF16),
        ),
        in_specs=[smem] + [vmem] * 11,
        out_specs=(vmem, vmem, vmem),
        scratch_shapes=[
            pltpu.VMEM((KPAD, 256), BF16),
            pltpu.VMEM((2, 56, HALF), F32),
            pltpu.VMEM((1, 256), F32),
            pltpu.VMEM((256, HB * HALF), F32),
            pltpu.VMEM((HB * HALF, 256), BF16),
            pltpu.VMEM((HB * HALF, 256), BF16),
            pltpu.VMEM((2, A_DEV * PROWS * PITCH, HALF), F32),
            pltpu.VMEM((2, cells, HALF), F32),
            pltpu.VMEM((2, 56, HALF), F32),
            pltpu.VMEM((cells, HALF), F32),
            pltpu.VMEM((256, cells), BF16),
            pltpu.VMEM((256, cells), BF16),
            pltpu.VMEM((HID, cells), BF16),
            pltpu.VMEM((HID, cells), BF16),
            pltpu.VMEM((256, TT), F32),
            pltpu.VMEM((2, cells, HALF), F32),
            pltpu.VMEM((C, HB * HALF), F32),
            pltpu.VMEM((C, HB * HALF), F32),
        ],
        compiler_params=pltpu.CompilerParams(vmem_limit_bytes=32 << 20),
        name="block",
    )(in_hbm(valid_rows), side, band, on_chip(near), on_chip(swap), inputs, stem_w, dw_kernel.T, in_hbm(norm_gain.reshape(1, C)), w_in, w_out.T, cotangent[0])

    arrived = lax.ppermute(send, "lat", siblings)
    chip_sum = (own + arrived.astype(F32)).astype(BF16)
    every = [[i * lon + j for i in range(c, lat, 2) for j in range(lon)] for c in range(2)]
    part = lax.all_to_all(chip_sum, ("lat", "lon"), 0, 0, axis_index_groups=every, tiled=True)
    part = jnp.sum(part.astype(F32), axis=0)
    whole = part.astype(BF16)
    spread = jnp.broadcast_to(whole[None], (CHUNKS, 24, HALF))
    spread = lax.all_to_all(spread, ("lat", "lon"), 0, 0, axis_index_groups=every, tiled=True)
    other = lax.ppermute(spread, "lat", siblings)
    win, wout, ker, gain = pl.pallas_call(
        final_kernel,
        out_shape=(
            jax.ShapeDtypeStruct((C, HID), F32),
            jax.ShapeDtypeStruct((C, HID), F32),
            jax.ShapeDtypeStruct((KW * KW, C), F32),
            jax.ShapeDtypeStruct((1, C), F32),
        ),
        in_specs=[vmem, vmem],
        out_specs=(vmem, vmem, vmem, vmem),
        scratch_shapes=[pltpu.VMEM((56, 256), F32)],
        compiler_params=pltpu.CompilerParams(vmem_limit_bytes=8 << 20),
        name="finish",
    )(on_chip(spread), on_chip(other))
    return out_tiles[None], win, wout.T, ker.T, gain.reshape(C)


def solution(mesh):
    tiles = P("lon", "lat", None, None)
    in_specs = (tiles, P("lon", "lat"), P("lon", "lat"), P(), P(), P(), P(), P(), tiles)
    out_specs = (tiles, P(), P(), P(), P())
    return jax.shard_map(body, mesh=mesh, in_specs=in_specs, out_specs=out_specs, check_vma=False)
```

```python
import jax
import jax.numpy as jnp
import numpy as np
from jax import lax
from jax.experimental import pallas as pl
from jax.experimental.pallas import tpu as pltpu
from jax.sharding import PartitionSpec as P

C = 200
CIN = 77
HID = 800
KW = 7
TS = 16
TT = 256
A_DEV = 4
COLS = 8
TILE_ROWS = 64
HALF = 128
KPAD = 80
PIECE = 48
SHELL = 160
PAY = A_DEV * SHELL
STRIP = 72
GROUP = 8
PITCH = 24
PROWS = TS + KW - 1
HB = 7
CHUNKS = 64
F32 = jnp.float32
BF16 = jnp.bfloat16
TN = (((0,), (0,)), ((), ()))
NT = (((1,), (1,)), ((), ()))
DIRS = [(dr, dc) for dr in (-1, 0, 1) for dc in (-1, 0, 1) if (dr, dc) != (0, 0)]


def shell_cells():
    m = np.arange(60)
    ends = (3 + m // 6) * TS + np.where(m % 6 < 3, m % 6, m % 6 + 10)
    cells = np.concatenate([np.arange(PIECE), 13 * TS + np.arange(PIECE), ends, np.full(100, -1)])
    return cells.reshape(1, 256).astype(np.int32)


def strip_sources():
    lane_of = {int(c): i for i, c in enumerate(shell_cells()[0]) if c >= 0}
    table = np.full((STRIP, HALF), -100000, np.int32)
    for j in range(3 * PROWS):
        row, c = j // 3 - 3, j % 3
        part = 0 if row < 0 else (1 if row < TS else 2)
        for side in range(2):
            table[j, 3 * side + part] = lane_of[(row % TS) * TS + (13 + c if side == 0 else c)]
    table[:PIECE, 6] = lane_of[13 * TS] + np.arange(PIECE)
    table[:PIECE, 7] = np.arange(PIECE)
    return table


def shell_kernel(pos_ref, rows_ref, x_ref, map_ref, shell_ref, kept_ref, flat, cut, buf):
    for k in range(CIN):
        for h in range(2):
            flat[h, A_DEV * k : A_DEV * k + A_DEV, :] = x_ref[k, :, h * HALF : (h + 1) * HALF].astype(F32)
    row = lax.broadcasted_iota(jnp.int32, (A_DEV * CIN, 1), 0) % A_DEV
    limit = jnp.full((A_DEV * CIN, 1), rows_ref[0, 0], jnp.int32)
    for a in range(1, A_DEV):
        limit = jnp.where(row == a, rows_ref[0, a], limit)
    cell_row = lax.broadcasted_iota(jnp.int32, (1, TT), 1) // TS
    for h in range(2):
        flat[h] = jnp.where(cell_row[:, h * HALF : (h + 1) * HALF] < limit, flat[h], 0.0)
    cell_id = lax.broadcasted_iota(jnp.int32, (TT, 256), 0)
    pick = (cell_id == map_ref[...]).astype(F32).astype(BF16)
    pieces = jnp.dot(flat[0].astype(BF16), pick[0:HALF], preferred_element_type=F32)
    pieces = pieces + jnp.dot(flat[1].astype(BF16), pick[HALF:TT], preferred_element_type=F32)
    cut[0] = pieces[:, 0:HALF]
    cut[1] = pieces[:, HALF:256]
    fill = lax.broadcasted_iota(jnp.int32, (3, 1), 0)
    kept_ref[...] = jnp.zeros_like(kept_ref)
    for a in range(A_DEV):
        for h in range(2):
            kept_ref[a, 0:CIN, h * HALF : (h + 1) * HALF] = flat[h, pl.ds(a, CIN, stride=A_DEV), :].astype(BF16)
        place = pos_ref[0, a]
        tail = jnp.where(fill == 0, place // 16, jnp.where(fill == 1, place % 16, 0)).astype(F32)
        at = a * SHELL
        buf[0:CIN, at : at + HALF] = cut[0, pl.ds(a, CIN, stride=A_DEV), :]
        buf[0:CIN, at + HALF : at + SHELL] = cut[1, pl.ds(a, CIN, stride=A_DEV), :][:, 0 : SHELL - HALF]
        buf[CIN:KPAD, at : at + SHELL] = jnp.broadcast_to(tail, (3, SHELL))
    shell_ref[...] = buf[...].astype(BF16)


def pick_kernel(
    pos_ref, far_pos_ref, ga_ref, gb_ref, src_ref,
    side_ref, band_ref, give_ref,
    pm, tv, sm, ts, sem, gaps,
):
    for g in range(GROUP):
        for j, ref in enumerate((ga_ref, gb_ref)):
            tail = ref[g, 64:KPAD, :].astype(F32)
            pm[2 * g + j : 2 * g + j + 1, :] = tail[13:14, :] * 16.0 + tail[14:15, :]
    lane = lax.broadcasted_iota(jnp.int32, (16, PAY), 1)
    slot = lax.broadcasted_iota(jnp.int32, (16, PAY), 0)
    label = jnp.where(lane % SHELL == 0, pm[...], -1.0)
    code = (slot * 1024 + lane + 1).astype(F32)
    tv[...] = jnp.zeros_like(tv)
    odd = lax.axis_index("lat") % 2
    near_edge = odd * (COLS - 1)

    def ask(entry, want):
        hit = jnp.where(label == want.astype(F32), code, 0.0)
        acc = jnp.sum(hit, axis=0, keepdims=True)
        folded = acc[:, 0:HALF]
        for i in range(1, PAY // HALF):
            folded = folded + acc[:, i * HALF : (i + 1) * HALF]
        tv[entry : entry + 1, :] = folded

    for a in range(A_DEV):
        q = pos_ref[0, a]
        row, col = q // COLS, q % COLS
        for n, (dr, dc) in enumerate(DIRS):
            nrow, ncol = row + dr, col + dc
            inside = (nrow >= 0) & (nrow < TILE_ROWS) & (ncol >= 0) & (ncol < COLS)
            ask(a * 8 + n, jnp.where(inside, nrow * COLS + ncol, -7))
        for first, i in ((32, 0), (48, 1)):
            q = far_pos_ref[i, a]
            row, col = q // COLS, q % COLS
            for dr in (-1, 0, 1):
                inside = (row + dr >= 0) & (row + dr < TILE_ROWS) & (col == near_edge)
                ask(first + a * 4 + dr + 1, jnp.where(inside, (row + dr) * COLS + COLS - 1 - near_edge, -7))
    total = jnp.sum(tv[...], axis=1, keepdims=True)
    sm[...] = jnp.broadcast_to(total, (64, HALF)).astype(jnp.int32)
    tcopy = pltpu.make_async_copy(sm, ts, sem)
    tcopy.start()
    column = lax.broadcasted_iota(jnp.int32, (STRIP, 256), 1)
    for n in range(8):
        gaps[n] = column - src_ref[:, n : n + 1]
    tcopy.wait()

    def take(entry, n, size):
        got = ts[entry, 0]
        spot = jnp.maximum(got - 1, 0)
        source = spot // 1024
        at = spot % 1024
        block = at // HALF
        shift = jnp.where(got == 0, -5000, at - block * HALF)
        cells = pl.ds(pl.multiple_of(block * HALF, HALF), 256)
        near = ga_ref[source // 2, :, cells]
        far = gb_ref[source // 2, :, cells]
        window = jnp.where(source % 2 == 0, near, far)
        pick = (gaps[n, 0:size, :] == shift).astype(F32).astype(BF16)
        return lax.dot_general(pick, window, NT, preferred_element_type=F32)

    order = {where: n for n, where in enumerate(DIRS)}
    for a in range(A_DEV):
        rows = slice(a * STRIP, (a + 1) * STRIP)
        for side, dc in enumerate((-1, 1)):
            parts = [take(a * 8 + order[dr, dc], 3 * side + dr + 1, STRIP) for dr in (-1, 0, 1)]
            side_ref[side, rows, :] = (parts[0] + parts[1] + parts[2]).astype(BF16)
        band_ref[2 * a] = take(a * 8 + order[-1, 0], 6, PIECE).astype(BF16)
        band_ref[2 * a + 1] = take(a * 8 + order[1, 0], 7, PIECE).astype(BF16)
        for i, first in ((0, 32), (1, 48)):
            parts = [take(first + a * 4 + dr + 1, 3 * odd + dr + 1, STRIP) for dr in (-1, 0, 1)]
            give_ref[i, rows, :] = (parts[0] + parts[1] + parts[2]).astype(BF16)


def gelu_parts(v):
    k = 0.7978845608028654
    sq = v * v
    u = 0.5 * jnp.tanh(v * (k + (k * 0.044715) * sq)) + 0.5
    value = v * u
    slope = u + (value - value * u) * (2.0 * k + (6.0 * k * 0.044715) * sq)
    return value, slope


def main_kernel(
    rows_ref, side_ref, band_ref, near_ref, swap_ref, x_ref, sw_ref, dw_ref, gain_ref, wi_ref, wo_ref, cot_ref,
    out_ref, own_ref, send_ref,
    swp, dwt, gnp, wide, wit, wot, pt, cv, un, iv, ft, mg, hs, gps, gf, gc, si, so,
):
    swp[...] = jnp.zeros_like(swp)
    swp[0:CIN, 0:C] = sw_ref[...]
    dwt[1] = jnp.zeros((56, HALF), F32)
    dwt[0, 0 : KW * KW, :] = dw_ref[:, 0:HALF]
    dwt[1, 0 : KW * KW, 0 : C - HALF] = dw_ref[:, HALF:C]
    gnp[...] = jnp.zeros_like(gnp)
    gnp[:, 0:C] = gain_ref[...]
    gain0 = gnp[:, 0:HALF]
    gain1 = gnp[:, HALF:256]

    for a in range(A_DEV):
        rows = lax.dot_general(x_ref[a], swp[...], TN, preferred_element_type=F32)
        rows = rows.astype(BF16).astype(F32)
        for h in range(2):
            for y in range(TS):
                at = (a * PROWS + 3 + y) * PITCH + 3
                pt[h, at : at + TS, :] = rows[y * TS : (y + 1) * TS, h * HALF : (h + 1) * HALF]
    cell_row = lax.broadcasted_iota(jnp.int32, (1, TT), 1) // TS
    mg[...] = jnp.zeros_like(mg)
    for a in range(A_DEV):
        keep = cell_row < rows_ref[0, a]
        mg[0:C, a * TT : (a + 1) * TT] = jnp.where(keep, cot_ref[a].astype(F32), 0.0).astype(BF16)
    wide[C:256, :] = jnp.zeros((256 - C, HB * HALF), F32)
    wide[:, 768:896] = jnp.zeros((256, HALF), F32)
    for src, dst in ((wi_ref, wit), (wo_ref, wot)):
        wide[0:C, 0:HID] = src[...].astype(F32)
        for b in range(HB):
            dst[b * HALF : (b + 1) * HALF, :] = wide[:, b * HALF : (b + 1) * HALF].T.astype(BF16)

    odd = lax.axis_index("lat") % 2 == 1
    near = near_ref[0].astype(F32)
    swap = swap_ref[1].astype(F32)
    for side, (even, other, xx) in enumerate(((near, swap, 0), (swap, near, 19))):
        arrived = jnp.where(odd, other, even)
        cells = (side_ref[side].astype(F32) + arrived).astype(BF16)
        rows = jnp.dot(cells, swp[...], preferred_element_type=F32).astype(BF16).astype(F32)
        for h in range(2):
            for a in range(A_DEV):
                for y in range(PROWS):
                    at = (a * PROWS + y) * PITCH + xx
                    j = a * STRIP + 3 * y
                    pt[h, at : at + 3, :] = rows[j : j + 3, h * HALF : (h + 1) * HALF]
    for a in range(A_DEV):
        for n in range(2):
            rows = jnp.dot(band_ref[2 * a + n], swp[...], preferred_element_type=F32).astype(BF16).astype(F32)
            for h in range(2):
                for i in range(3):
                    at = (a * PROWS + 19 * n + i) * PITCH + 3
                    pt[h, at : at + TS, :] = rows[i * TS : (i + 1) * TS, h * HALF : (h + 1) * HALF]

    def conv_step(step, carry):
        h = step // (2 * A_DEV)
        part = step % (2 * A_DEV)
        at = pl.multiple_of((part // 2) * (PROWS * PITCH) + (part % 2) * (8 * PITCH), 8)
        acc = [jnp.zeros((TS, HALF), F32) for _ in range(8)]
        for r in range(KW):
            for k in range(KW):
                w = jnp.broadcast_to(dwt[h, r * KW + k : r * KW + k + 1, :], (TS, HALF))
                for y in range(8):
                    acc[y] = acc[y] + w * pt[h, pl.ds(at + (y + r) * PITCH + k, TS), :]
        for y in range(8):
            cv[h, pl.ds(pl.multiple_of(part * HALF, 8) + y * TS, TS), :] = acc[y]
        return carry

    lax.fori_loop(0, 4 * A_DEV, conv_step, 0)

    live = lax.broadcasted_iota(jnp.int32, (1, HALF), 1) < C - HALF
    for a in range(A_DEV):
        span = slice(a * TT, (a + 1) * TT)
        c0 = cv[0, span, :]
        c1 = cv[1, span, :]
        mean = jnp.sum(c0 + c1, axis=1, keepdims=True) * (1.0 / C)
        c0 = c0 - mean
        c1 = jnp.where(live, c1 - mean, 0.0)
        inv = lax.rsqrt(jnp.sum(c0 * c0 + c1 * c1, axis=1, keepdims=True) * (1.0 / C) + 1e-6)
        u0 = c0 * inv
        u1 = c1 * inv
        cv[0, span, :] = u0
        cv[1, span, :] = u1
        iv[span, :] = jnp.broadcast_to(inv, (TT, HALF))
        ft[0:HALF, span] = (u0 * gain0).T.astype(BF16)
        ft[HALF:256, span] = (u1 * gain1).T.astype(BF16)

    for b in range(HID // 80):
        span = slice(b * 80, (b + 1) * 80)
        preact = jnp.dot(wit[span, :], ft[...], preferred_element_type=F32)
        grad_hidden = jnp.dot(wot[span, :], mg[...], preferred_element_type=F32)
        value, slope = gelu_parts(preact)
        hs[span, :] = value.astype(BF16)
        gps[span, :] = (grad_hidden * slope).astype(BF16)
    gf[C:256, :] = jnp.zeros((256 - C, TT), F32)
    sums = [jnp.zeros((1, HALF), F32), jnp.zeros((1, HALF), F32)]
    for a in range(A_DEV):
        span = slice(a * TT, (a + 1) * TT)
        gf[0:C, :] = jnp.dot(wi_ref[...], gps[:, span], preferred_element_type=F32)
        g0 = gf[0:HALF, :].T.astype(BF16).astype(F32)
        g1 = gf[HALF:256, :].T.astype(BF16).astype(F32)
        u0 = cv[0, span, :]
        u1 = cv[1, span, :]
        inv = iv[span, :]
        sums[0] = sums[0] + jnp.sum(g0 * u0, axis=0, keepdims=True)
        sums[1] = sums[1] + jnp.sum(g1 * u1, axis=0, keepdims=True)
        d0 = g0 * gain0
        d1 = g1 * gain1
        m1 = jnp.sum(d0 + d1, axis=1, keepdims=True) * (1.0 / C)
        m2 = jnp.sum(d0 * u0 + d1 * u1, axis=1, keepdims=True) * (1.0 / C)
        gc[0, span, :] = inv * (d0 - m1 - u0 * m2)
        gc[1, span, :] = jnp.where(live, inv * (d1 - m1 - u1 * m2), 0.0)
        stem = lax.dot_general(swp[...], x_ref[a], TN, preferred_element_type=F32)[0:C, :].astype(BF16).astype(F32)
        branch = jnp.dot(wo_ref[...], hs[:, span], preferred_element_type=F32)
        keep = cell_row < rows_ref[0, a]
        out_ref[a] = jnp.where(keep, branch + stem, 0.0).astype(BF16)
    si[:, 768:896] = jnp.zeros((C, HALF), F32)
    so[:, 768:896] = jnp.zeros((C, HALF), F32)
    si[:, 0:HID] = lax.dot_general(ft[0:C, :], gps[...], NT, preferred_element_type=F32)
    so[:, 0:HID] = lax.dot_general(mg[0:C, :], hs[...], NT, preferred_element_type=F32)

    un[0, 48:56, :] = jnp.zeros((8, HALF), F32)
    un[1, 48:56, :] = jnp.zeros((8, HALF), F32)

    def tap_step(step, carry):
        h = step % 2
        r = step // 2
        down = pl.multiple_of(r * PITCH, 8)
        def tile_step(a, acc):
            acc = list(acc)
            at = pl.multiple_of(a * (PROWS * PITCH) + down, 8)
            for y in range(TS):
                g = gc[h, pl.ds(pl.multiple_of(a * TT, 8) + y * TS, TS), :]
                for k in range(KW):
                    acc[k] = acc[k] + g * pt[h, pl.ds(at + y * PITCH + k, TS), :]
            return tuple(acc)

        acc = lax.fori_loop(0, A_DEV, tile_step, tuple(jnp.zeros((TS, HALF), F32) for _ in range(KW)))
        for k in range(KW):
            un[h, pl.ds(r * KW + k, 1), :] = jnp.sum(acc[k], axis=0, keepdims=True)
        return carry

    lax.fori_loop(0, 2 * KW, tap_step, 0)
    un[0, 49:50, :] = sums[0]
    un[1, 49:50, :] = sums[1]

    lat_id = lax.axis_index("lat")
    is_low = lat_id % 2 == 0
    device = lat_id * lax.axis_size("lon") + lax.axis_index("lon")
    blank = jnp.zeros((8, HALF), F32)
    count = ((rows_ref[0, 0] + rows_ref[0, 1] + rows_ref[0, 2] + rows_ref[0, 3]) * TS).astype(F32)

    def blocks(t):
        if t < 25 * HB:
            r, b = t // HB, t % HB
            return si[8 * r : 8 * r + 8, b * HALF : (b + 1) * HALF], so[8 * r : 8 * r + 8, b * HALF : (b + 1) * HALF]
        t = t - 25 * HB
        if t < 14:
            return un[t // HB, 8 * (t % HB) : 8 * (t % HB) + 8, :], blank
        if t == 14:
            return jnp.where(lax.broadcasted_iota(jnp.int32, (8, HALF), 1) == device, count, blank), blank
        return blank, blank

    for chunk in range(CHUNKS):
        pairs = [blocks(3 * chunk + i) for i in range(3)]
        for i, (low, high) in enumerate(pairs):
            own_ref[chunk, 8 * i : 8 * i + 8, :] = jnp.where(is_low, low, high)
        sent = jnp.concatenate([jnp.where(is_low, high, low) for low, high in pairs], axis=0)
        send_ref[chunk] = sent.astype(BF16)


def final_kernel(own_ref, other_ref, win_ref, wout_ref, ker_ref, gain_ref, ks):
    is_low = lax.axis_index("lat") % 2 == 0

    def pair(chunk):
        own = own_ref[chunk].astype(F32)
        other = other_ref[chunk].astype(F32)
        return jnp.where(is_low, own, other), jnp.where(is_low, other, own)

    scale = 1.0 / jnp.sum(pair(CHUNKS - 1)[0][0:1, :], axis=1, keepdims=True)
    for chunk in range(CHUNKS - 1):
        low, high = pair(chunk)
        for i in range(3):
            t = 3 * chunk + i
            block = low[8 * i : 8 * i + 8, :] * scale
            if t < 25 * HB:
                r, b = t // HB, t % HB
                wide = HALF if b < HB - 1 else HID - (HB - 1) * HALF
                win_ref[8 * r : 8 * r + 8, b * HALF : b * HALF + wide] = block[:, 0:wide]
                turned = high[8 * i : 8 * i + 8, :] * scale
                wout_ref[8 * r : 8 * r + 8, b * HALF : b * HALF + wide] = turned[:, 0:wide]
            else:
                t = t - 25 * HB
                ks[8 * (t % HB) : 8 * (t % HB) + 8, (t // HB) * HALF : (t // HB + 1) * HALF] = block
    ker_ref[...] = ks[0 : KW * KW, 0:C]
    gain_ref[...] = ks[49:50, 0:C]


def on_chip(value):
    return pltpu.with_memory_space_constraint(value, pltpu.VMEM)


def in_hbm(value):
    return pltpu.with_memory_space_constraint(value, pltpu.HBM)


def body(x_tiles, tile_pos, valid_rows, stem_w, dw_kernel, norm_gain, w_in, w_out, cotangent):
    smem = pl.BlockSpec(memory_space=pltpu.SMEM)
    vmem = pl.BlockSpec(memory_space=pltpu.VMEM)
    lon = lax.axis_size("lon")
    lat = lax.axis_size("lat")
    hop = [(i * lon + j, i * lon + (j + (1 if i % 2 == 0 else -1)) % lon) for i in range(lat) for j in range(lon)]
    back = [(target, source) for source, target in hop]
    siblings = [(i, i ^ 1) for i in range(lat)]
    pos_pair = jnp.concatenate([tile_pos, lax.ppermute(tile_pos, "lat", siblings)], axis=0)
    pos_far = lax.ppermute(pos_pair, ("lat", "lon"), back)
    shell, inputs = pl.pallas_call(
        shell_kernel,
        out_shape=(pltpu.VMEM((KPAD, PAY), BF16), pltpu.VMEM((A_DEV, KPAD, TT), BF16)),
        in_specs=[smem, smem, vmem, vmem],
        out_specs=(vmem, vmem),
        scratch_shapes=[
            pltpu.VMEM((2, A_DEV * CIN, HALF), F32),
            pltpu.VMEM((2, A_DEV * CIN, HALF), F32),
            pltpu.VMEM((KPAD, PAY), F32),
        ],
        name="shell",
    )(tile_pos, valid_rows, x_tiles[0].transpose(1, 0, 2), jnp.asarray(shell_cells()))
    shell, pos_far = lax.optimization_barrier((shell, pos_far))
    same_core = [[i for i in range(c, lat, 2)] for c in range(2)]
    mine = lax.all_to_all(
        jnp.broadcast_to(shell[None], (GROUP, KPAD, PAY)), "lat", 0, 0, axis_index_groups=same_core, tiled=True
    )
    theirs = lax.ppermute(mine, "lat", siblings)
    side, band, give = pl.pallas_call(
        pick_kernel,
        out_shape=(
            pltpu.VMEM((2, A_DEV * STRIP, KPAD), BF16),
            pltpu.VMEM((2 * A_DEV, PIECE, KPAD), BF16),
            pltpu.VMEM((2, A_DEV * STRIP, KPAD), BF16),
        ),
        in_specs=[smem] * 2 + [vmem] * 3,
        out_specs=(vmem, vmem, vmem),
        scratch_shapes=[
            pltpu.VMEM((16, PAY), F32),
            pltpu.VMEM((64, HALF), F32),
            pltpu.VMEM((64, HALF), jnp.int32),
            pltpu.SMEM((64, HALF), jnp.int32),
            pltpu.SemaphoreType.DMA,
            pltpu.VMEM((8, STRIP, 256), jnp.int32),
        ],
        compiler_params=pltpu.CompilerParams(vmem_limit_bytes=16 << 20),
        name="pick",
    )(tile_pos, pos_far, on_chip(mine), on_chip(theirs), jnp.asarray(strip_sources()))
    near = lax.ppermute(give, ("lat", "lon"), hop)
    swap = lax.ppermute(near, "lat", siblings)

    cells = A_DEV * TT
    out_tiles, own, send = pl.pallas_call(
        main_kernel,
        out_shape=(
            jax.ShapeDtypeStruct((A_DEV, C, TT), BF16),
            pltpu.VMEM((CHUNKS, 24, HALF), F32),
            pltpu.VMEM((CHUNKS, 24, HALF), BF16),
        ),
        in_specs=[smem] + [vmem] * 11,
        out_specs=(vmem, vmem, vmem),
        scratch_shapes=[
            pltpu.VMEM((KPAD, 256), BF16),
            pltpu.VMEM((2, 56, HALF), F32),
            pltpu.VMEM((1, 256), F32),
            pltpu.VMEM((256, HB * HALF), F32),
            pltpu.VMEM((HB * HALF, 256), BF16),
            pltpu.VMEM((HB * HALF, 256), BF16),
            pltpu.VMEM((2, A_DEV * PROWS * PITCH, HALF), F32),
            pltpu.VMEM((2, cells, HALF), F32),
            pltpu.VMEM((2, 56, HALF), F32),
            pltpu.VMEM((cells, HALF), F32),
            pltpu.VMEM((256, cells), BF16),
            pltpu.VMEM((256, cells), BF16),
            pltpu.VMEM((HID, cells), BF16),
            pltpu.VMEM((HID, cells), BF16),
            pltpu.VMEM((256, TT), F32),
            pltpu.VMEM((2, cells, HALF), F32),
            pltpu.VMEM((C, HB * HALF), F32),
            pltpu.VMEM((C, HB * HALF), F32),
        ],
        compiler_params=pltpu.CompilerParams(vmem_limit_bytes=32 << 20),
        name="block",
    )(in_hbm(valid_rows), side, band, on_chip(near), on_chip(swap), inputs, stem_w, dw_kernel.T, in_hbm(norm_gain.reshape(1, C)), w_in, w_out.T, cotangent[0])

    arrived = lax.ppermute(send, "lat", siblings)
    chip_sum = (own + arrived.astype(F32)).astype(BF16)
    every = [[i * lon + j for i in range(c, lat, 2) for j in range(lon)] for c in range(2)]
    part = lax.all_to_all(chip_sum, ("lat", "lon"), 0, 0, axis_index_groups=every, tiled=True)
    part = jnp.sum(part.astype(F32), axis=0)
    whole = part.astype(BF16)
    spread = jnp.broadcast_to(whole[None], (CHUNKS, 24, HALF))
    spread = lax.all_to_all(spread, ("lat", "lon"), 0, 0, axis_index_groups=every, tiled=True)
    other = lax.ppermute(spread, "lat", siblings)
    win, wout, ker, gain = pl.pallas_call(
        final_kernel,
        out_shape=(
            jax.ShapeDtypeStruct((C, HID), F32),
            jax.ShapeDtypeStruct((C, HID), F32),
            jax.ShapeDtypeStruct((KW * KW, C), F32),
            jax.ShapeDtypeStruct((1, C), F32),
        ),
        in_specs=[vmem, vmem],
        out_specs=(vmem, vmem, vmem, vmem),
        scratch_shapes=[pltpu.VMEM((56, 256), F32)],
        compiler_params=pltpu.CompilerParams(vmem_limit_bytes=8 << 20),
        name="finish",
    )(on_chip(spread), on_chip(other))
    return out_tiles[None], win, wout.T, ker.T, gain.reshape(C)


def solution(mesh):
    tiles = P("lon", "lat", None, None)
    in_specs = (tiles, P("lon", "lat"), P("lon", "lat"), P(), P(), P(), P(), P(), tiles)
    out_specs = (tiles, P(), P(), P(), P())
    return jax.shard_map(body, mesh=mesh, in_specs=in_specs, out_specs=out_specs, check_vma=False)
```

```python
import jax
import jax.numpy as jnp
import numpy as np
from jax import lax
from jax.experimental import pallas as pl
from jax.experimental.pallas import tpu as pltpu
from jax.sharding import PartitionSpec as P

C = 200
CIN = 77
HID = 800
KW = 7
TS = 16
TT = 256
A_DEV = 4
COLS = 8
TILE_ROWS = 64
HALF = 128
KPAD = 80
PIECE = 48
SHELL = 160
PAY = A_DEV * SHELL
STRIP = 72
GROUP = 8
PITCH = 24
PROWS = TS + KW - 1
HB = 7
CHUNKS = 64
F32 = jnp.float32
BF16 = jnp.bfloat16
TN = (((0,), (0,)), ((), ()))
NT = (((1,), (1,)), ((), ()))
DIRS = [(dr, dc) for dr in (-1, 0, 1) for dc in (-1, 0, 1) if (dr, dc) != (0, 0)]


def shell_cells():
    m = np.arange(60)
    ends = (3 + m // 6) * TS + np.where(m % 6 < 3, m % 6, m % 6 + 10)
    cells = np.concatenate([np.arange(PIECE), 13 * TS + np.arange(PIECE), ends, np.full(100, -1)])
    return cells.reshape(1, 256).astype(np.int32)


def strip_sources():
    lane_of = {int(c): i for i, c in enumerate(shell_cells()[0]) if c >= 0}
    table = np.full((STRIP, HALF), -100000, np.int32)
    for j in range(3 * PROWS):
        row, c = j // 3 - 3, j % 3
        part = 0 if row < 0 else (1 if row < TS else 2)
        for side in range(2):
            table[j, 3 * side + part] = lane_of[(row % TS) * TS + (13 + c if side == 0 else c)]
    table[:PIECE, 6] = lane_of[13 * TS] + np.arange(PIECE)
    table[:PIECE, 7] = np.arange(PIECE)
    return table


def shell_kernel(pos_ref, rows_ref, x_ref, map_ref, shell_ref, kept_ref, flat, cut, buf):
    for k in range(CIN):
        for h in range(2):
            flat[h, A_DEV * k : A_DEV * k + A_DEV, :] = x_ref[k, :, h * HALF : (h + 1) * HALF].astype(F32)
    row = lax.broadcasted_iota(jnp.int32, (A_DEV * CIN, 1), 0) % A_DEV
    limit = jnp.full((A_DEV * CIN, 1), rows_ref[0, 0], jnp.int32)
    for a in range(1, A_DEV):
        limit = jnp.where(row == a, rows_ref[0, a], limit)
    cell_row = lax.broadcasted_iota(jnp.int32, (1, TT), 1) // TS
    for h in range(2):
        flat[h] = jnp.where(cell_row[:, h * HALF : (h + 1) * HALF] < limit, flat[h], 0.0)
    cell_id = lax.broadcasted_iota(jnp.int32, (TT, 256), 0)
    pick = (cell_id == map_ref[...]).astype(F32).astype(BF16)
    pieces = jnp.dot(flat[0].astype(BF16), pick[0:HALF], preferred_element_type=F32)
    pieces = pieces + jnp.dot(flat[1].astype(BF16), pick[HALF:TT], preferred_element_type=F32)
    cut[0] = pieces[:, 0:HALF]
    cut[1] = pieces[:, HALF:256]
    fill = lax.broadcasted_iota(jnp.int32, (3, 1), 0)
    kept_ref[...] = jnp.zeros_like(kept_ref)
    for a in range(A_DEV):
        for h in range(2):
            kept_ref[a, 0:CIN, h * HALF : (h + 1) * HALF] = flat[h, pl.ds(a, CIN, stride=A_DEV), :].astype(BF16)
        place = pos_ref[0, a]
        tail = jnp.where(fill == 0, place // 16, jnp.where(fill == 1, place % 16, 0)).astype(F32)
        at = a * SHELL
        buf[0:CIN, at : at + HALF] = cut[0, pl.ds(a, CIN, stride=A_DEV), :]
        buf[0:CIN, at + HALF : at + SHELL] = cut[1, pl.ds(a, CIN, stride=A_DEV), :][:, 0 : SHELL - HALF]
        buf[CIN:KPAD, at : at + SHELL] = jnp.broadcast_to(tail, (3, SHELL))
    shell_ref[...] = buf[...].astype(BF16)


def pick_kernel(
    pos_ref, far_pos_ref, ga_ref, gb_ref, src_ref,
    side_ref, band_ref, give_ref,
    pm, tv, sm, ts, sem, gaps,
):
    for g in range(GROUP):
        for j, ref in enumerate((ga_ref, gb_ref)):
            tail = ref[g, 64:KPAD, :].astype(F32)
            pm[2 * g + j : 2 * g + j + 1, :] = tail[13:14, :] * 16.0 + tail[14:15, :]
    lane = lax.broadcasted_iota(jnp.int32, (16, PAY), 1)
    slot = lax.broadcasted_iota(jnp.int32, (16, PAY), 0)
    label = jnp.where(lane % SHELL == 0, pm[...], -1.0)
    code = (slot * 1024 + lane + 1).astype(F32)
    tv[...] = jnp.zeros_like(tv)
    odd = lax.axis_index("lat") % 2
    near_edge = odd * (COLS - 1)

    def ask(entry, want):
        hit = jnp.where(label == want.astype(F32), code, 0.0)
        acc = jnp.sum(hit, axis=0, keepdims=True)
        folded = acc[:, 0:HALF]
        for i in range(1, PAY // HALF):
            folded = folded + acc[:, i * HALF : (i + 1) * HALF]
        tv[entry : entry + 1, :] = folded

    for a in range(A_DEV):
        q = pos_ref[0, a]
        row, col = q // COLS, q % COLS
        for n, (dr, dc) in enumerate(DIRS):
            nrow, ncol = row + dr, col + dc
            inside = (nrow >= 0) & (nrow < TILE_ROWS) & (ncol >= 0) & (ncol < COLS)
            ask(a * 8 + n, jnp.where(inside, nrow * COLS + ncol, -7))
        for first, i in ((32, 0), (48, 1)):
            q = far_pos_ref[i, a]
            row, col = q // COLS, q % COLS
            for dr in (-1, 0, 1):
                inside = (row + dr >= 0) & (row + dr < TILE_ROWS) & (col == near_edge)
                ask(first + a * 4 + dr + 1, jnp.where(inside, (row + dr) * COLS + COLS - 1 - near_edge, -7))
    total = jnp.sum(tv[...], axis=1, keepdims=True)
    sm[...] = jnp.broadcast_to(total, (64, HALF)).astype(jnp.int32)
    tcopy = pltpu.make_async_copy(sm, ts, sem)
    tcopy.start()
    column = lax.broadcasted_iota(jnp.int32, (STRIP, 256), 1)
    for n in range(8):
        gaps[n] = column - src_ref[:, n : n + 1]
    tcopy.wait()

    def take(entry, n, size):
        got = ts[entry, 0]
        spot = jnp.maximum(got - 1, 0)
        source = spot // 1024
        at = spot % 1024
        block = at // HALF
        shift = jnp.where(got == 0, -5000, at - block * HALF)
        cells = pl.ds(pl.multiple_of(block * HALF, HALF), 256)
        near = ga_ref[source // 2, :, cells]
        far = gb_ref[source // 2, :, cells]
        window = jnp.where(source % 2 == 0, near, far)
        pick = (gaps[n, 0:size, :] == shift).astype(F32).astype(BF16)
        return lax.dot_general(pick, window, NT, preferred_element_type=F32)

    order = {where: n for n, where in enumerate(DIRS)}
    for a in range(A_DEV):
        rows = slice(a * STRIP, (a + 1) * STRIP)
        for side, dc in enumerate((-1, 1)):
            parts = [take(a * 8 + order[dr, dc], 3 * side + dr + 1, STRIP) for dr in (-1, 0, 1)]
            side_ref[side, rows, :] = (parts[0] + parts[1] + parts[2]).astype(BF16)
        band_ref[2 * a] = take(a * 8 + order[-1, 0], 6, PIECE).astype(BF16)
        band_ref[2 * a + 1] = take(a * 8 + order[1, 0], 7, PIECE).astype(BF16)
        for i, first in ((0, 32), (1, 48)):
            parts = [take(first + a * 4 + dr + 1, 3 * odd + dr + 1, STRIP) for dr in (-1, 0, 1)]
            give_ref[i, rows, :] = (parts[0] + parts[1] + parts[2]).astype(BF16)


def gelu_parts(v):
    k = 0.7978845608028654
    sq = v * v
    u = 0.5 * jnp.tanh(v * (k + (k * 0.044715) * sq)) + 0.5
    value = v * u
    slope = u + (value - value * u) * (2.0 * k + (6.0 * k * 0.044715) * sq)
    return value, slope


def main_kernel(
    rows_ref, side_ref, band_ref, near_ref, swap_ref, x_ref, sw_ref, dw_ref, gain_ref, wi_ref, wo_ref, cot_ref,
    out_ref, own_ref, send_ref,
    swp, dwt, gnp, wide, wit, wot, pt, cv, un, iv, ft, mg, hs, gps, gf, gc, si, so,
):
    swp[...] = jnp.zeros_like(swp)
    swp[0:CIN, 0:C] = sw_ref[...]
    dwt[1] = jnp.zeros((56, HALF), F32)
    dwt[0, 0 : KW * KW, :] = dw_ref[:, 0:HALF]
    dwt[1, 0 : KW * KW, 0 : C - HALF] = dw_ref[:, HALF:C]
    gnp[...] = jnp.zeros_like(gnp)
    gnp[:, 0:C] = gain_ref[...]
    gain0 = gnp[:, 0:HALF]
    gain1 = gnp[:, HALF:256]

    for a in range(A_DEV):
        rows = lax.dot_general(x_ref[a], swp[...], TN, preferred_element_type=F32)
        rows = rows.astype(BF16).astype(F32)
        for h in range(2):
            for y in range(TS):
                at = (a * PROWS + 3 + y) * PITCH + 3
                pt[h, at : at + TS, :] = rows[y * TS : (y + 1) * TS, h * HALF : (h + 1) * HALF]
    cell_row = lax.broadcasted_iota(jnp.int32, (1, TT), 1) // TS
    mg[...] = jnp.zeros_like(mg)
    for a in range(A_DEV):
        keep = cell_row < rows_ref[0, a]
        mg[0:C, a * TT : (a + 1) * TT] = jnp.where(keep, cot_ref[a].astype(F32), 0.0).astype(BF16)
    wide[C:256, :] = jnp.zeros((256 - C, HB * HALF), F32)
    wide[:, 768:896] = jnp.zeros((256, HALF), F32)
    for src, dst in ((wi_ref, wit), (wo_ref, wot)):
        wide[0:C, 0:HID] = src[...].astype(F32)
        for b in range(HB):
            dst[b * HALF : (b + 1) * HALF, :] = wide[:, b * HALF : (b + 1) * HALF].T.astype(BF16)

    odd = lax.axis_index("lat") % 2 == 1
    near = near_ref[0].astype(F32)
    swap = swap_ref[1].astype(F32)
    for side, (even, other, xx) in enumerate(((near, swap, 0), (swap, near, 19))):
        arrived = jnp.where(odd, other, even)
        cells = (side_ref[side].astype(F32) + arrived).astype(BF16)
        rows = jnp.dot(cells, swp[...], preferred_element_type=F32).astype(BF16).astype(F32)
        for h in range(2):
            for a in range(A_DEV):
                for y in range(PROWS):
                    at = (a * PROWS + y) * PITCH + xx
                    j = a * STRIP + 3 * y
                    pt[h, at : at + 3, :] = rows[j : j + 3, h * HALF : (h + 1) * HALF]
    for a in range(A_DEV):
        for n in range(2):
            rows = jnp.dot(band_ref[2 * a + n], swp[...], preferred_element_type=F32).astype(BF16).astype(F32)
            for h in range(2):
                for i in range(3):
                    at = (a * PROWS + 19 * n + i) * PITCH + 3
                    pt[h, at : at + TS, :] = rows[i * TS : (i + 1) * TS, h * HALF : (h + 1) * HALF]

    def conv_step(step, carry):
        h = step // (2 * A_DEV)
        part = step % (2 * A_DEV)
        at = pl.multiple_of((part // 2) * (PROWS * PITCH) + (part % 2) * (8 * PITCH), 8)
        acc = [None] * 8
        for r in range(KW):
            for k in range(KW):
                w = jnp.broadcast_to(dwt[h, r * KW + k : r * KW + k + 1, :], (TS, HALF))
                for y in range(8):
                    term = w * pt[h, pl.ds(at + (y + r) * PITCH + k, TS), :]
                    acc[y] = term if acc[y] is None else acc[y] + term
        for y in range(8):
            cv[h, pl.ds(pl.multiple_of(part * HALF, 8) + y * TS, TS), :] = acc[y]
        return carry

    lax.fori_loop(0, 4 * A_DEV, conv_step, 0)

    live = lax.broadcasted_iota(jnp.int32, (1, HALF), 1) < C - HALF
    for a in range(A_DEV):
        span = slice(a * TT, (a + 1) * TT)
        c0 = cv[0, span, :]
        c1 = cv[1, span, :]
        mean = jnp.sum(c0 + c1, axis=1, keepdims=True) * (1.0 / C)
        c0 = c0 - mean
        c1 = jnp.where(live, c1 - mean, 0.0)
        inv = lax.rsqrt(jnp.sum(c0 * c0 + c1 * c1, axis=1, keepdims=True) * (1.0 / C) + 1e-6)
        u0 = c0 * inv
        u1 = c1 * inv
        cv[0, span, :] = u0
        cv[1, span, :] = u1
        iv[span, :] = jnp.broadcast_to(inv, (TT, HALF))
        ft[0:HALF, span] = (u0 * gain0).T.astype(BF16)
        ft[HALF:256, span] = (u1 * gain1).T.astype(BF16)

    for b in range(HID // 80):
        span = slice(b * 80, (b + 1) * 80)
        preact = jnp.dot(wit[span, :], ft[...], preferred_element_type=F32)
        grad_hidden = jnp.dot(wot[span, :], mg[...], preferred_element_type=F32)
        value, slope = gelu_parts(preact)
        hs[span, :] = value.astype(BF16)
        gps[span, :] = (grad_hidden * slope).astype(BF16)
    gf[C:256, :] = jnp.zeros((256 - C, TT), F32)
    sums = [jnp.zeros((1, HALF), F32), jnp.zeros((1, HALF), F32)]
    for a in range(A_DEV):
        span = slice(a * TT, (a + 1) * TT)
        gf[0:C, :] = jnp.dot(wi_ref[...], gps[:, span], preferred_element_type=F32)
        g0 = gf[0:HALF, :].T.astype(BF16).astype(F32)
        g1 = gf[HALF:256, :].T.astype(BF16).astype(F32)
        u0 = cv[0, span, :]
        u1 = cv[1, span, :]
        inv = iv[span, :]
        sums[0] = sums[0] + jnp.sum(g0 * u0, axis=0, keepdims=True)
        sums[1] = sums[1] + jnp.sum(g1 * u1, axis=0, keepdims=True)
        d0 = g0 * gain0
        d1 = g1 * gain1
        m1 = jnp.sum(d0 + d1, axis=1, keepdims=True) * (1.0 / C)
        m2 = jnp.sum(d0 * u0 + d1 * u1, axis=1, keepdims=True) * (1.0 / C)
        gc[0, span, :] = inv * (d0 - m1 - u0 * m2)
        gc[1, span, :] = jnp.where(live, inv * (d1 - m1 - u1 * m2), 0.0)
        stem = lax.dot_general(swp[...], x_ref[a], TN, preferred_element_type=F32)[0:C, :].astype(BF16).astype(F32)
        branch = jnp.dot(wo_ref[...], hs[:, span], preferred_element_type=F32)
        keep = cell_row < rows_ref[0, a]
        out_ref[a] = jnp.where(keep, branch + stem, 0.0).astype(BF16)
    si[:, 768:896] = jnp.zeros((C, HALF), F32)
    so[:, 768:896] = jnp.zeros((C, HALF), F32)
    si[:, 0:HID] = lax.dot_general(ft[0:C, :], gps[...], NT, preferred_element_type=F32)
    so[:, 0:HID] = lax.dot_general(mg[0:C, :], hs[...], NT, preferred_element_type=F32)

    un[0, 48:56, :] = jnp.zeros((8, HALF), F32)
    un[1, 48:56, :] = jnp.zeros((8, HALF), F32)

    def tap_step(step, carry):
        h = step % 2
        r = step // 2
        down = pl.multiple_of(r * PITCH, 8)
        def tile_step(a, acc):
            acc = list(acc)
            at = pl.multiple_of(a * (PROWS * PITCH) + down, 8)
            for y in range(TS):
                g = gc[h, pl.ds(pl.multiple_of(a * TT, 8) + y * TS, TS), :]
                for k in range(KW):
                    acc[k] = acc[k] + g * pt[h, pl.ds(at + y * PITCH + k, TS), :]
            return tuple(acc)

        acc = lax.fori_loop(0, A_DEV, tile_step, tuple(jnp.zeros((TS, HALF), F32) for _ in range(KW)))
        for k in range(KW):
            un[h, pl.ds(r * KW + k, 1), :] = jnp.sum(acc[k], axis=0, keepdims=True)
        return carry

    lax.fori_loop(0, 2 * KW, tap_step, 0)
    un[0, 49:50, :] = sums[0]
    un[1, 49:50, :] = sums[1]

    lat_id = lax.axis_index("lat")
    is_low = lat_id % 2 == 0
    device = lat_id * lax.axis_size("lon") + lax.axis_index("lon")
    blank = jnp.zeros((8, HALF), F32)
    count = ((rows_ref[0, 0] + rows_ref[0, 1] + rows_ref[0, 2] + rows_ref[0, 3]) * TS).astype(F32)

    def blocks(t):
        if t < 25 * HB:
            r, b = t // HB, t % HB
            return si[8 * r : 8 * r + 8, b * HALF : (b + 1) * HALF], so[8 * r : 8 * r + 8, b * HALF : (b + 1) * HALF]
        t = t - 25 * HB
        if t < 14:
            return un[t // HB, 8 * (t % HB) : 8 * (t % HB) + 8, :], blank
        if t == 14:
            return jnp.where(lax.broadcasted_iota(jnp.int32, (8, HALF), 1) == device, count, blank), blank
        return blank, blank

    for chunk in range(CHUNKS):
        pairs = [blocks(3 * chunk + i) for i in range(3)]
        for i, (low, high) in enumerate(pairs):
            own_ref[chunk, 8 * i : 8 * i + 8, :] = jnp.where(is_low, low, high)
        sent = jnp.concatenate([jnp.where(is_low, high, low) for low, high in pairs], axis=0)
        send_ref[chunk] = sent.astype(BF16)


def final_kernel(own_ref, other_ref, win_ref, wout_ref, ker_ref, gain_ref, ks):
    is_low = lax.axis_index("lat") % 2 == 0

    def pair(chunk):
        own = own_ref[chunk].astype(F32)
        other = other_ref[chunk].astype(F32)
        return jnp.where(is_low, own, other), jnp.where(is_low, other, own)

    scale = 1.0 / jnp.sum(pair(CHUNKS - 1)[0][0:1, :], axis=1, keepdims=True)
    for chunk in range(CHUNKS - 1):
        low, high = pair(chunk)
        for i in range(3):
            t = 3 * chunk + i
            block = low[8 * i : 8 * i + 8, :] * scale
            if t < 25 * HB:
                r, b = t // HB, t % HB
                wide = HALF if b < HB - 1 else HID - (HB - 1) * HALF
                win_ref[8 * r : 8 * r + 8, b * HALF : b * HALF + wide] = block[:, 0:wide]
                turned = high[8 * i : 8 * i + 8, :] * scale
                wout_ref[8 * r : 8 * r + 8, b * HALF : b * HALF + wide] = turned[:, 0:wide]
            else:
                t = t - 25 * HB
                ks[8 * (t % HB) : 8 * (t % HB) + 8, (t // HB) * HALF : (t // HB + 1) * HALF] = block
    ker_ref[...] = ks[0 : KW * KW, 0:C]
    gain_ref[...] = ks[49:50, 0:C]


def on_chip(value):
    return pltpu.with_memory_space_constraint(value, pltpu.VMEM)


def in_hbm(value):
    return pltpu.with_memory_space_constraint(value, pltpu.HBM)


def body(x_tiles, tile_pos, valid_rows, stem_w, dw_kernel, norm_gain, w_in, w_out, cotangent):
    smem = pl.BlockSpec(memory_space=pltpu.SMEM)
    vmem = pl.BlockSpec(memory_space=pltpu.VMEM)
    lon = lax.axis_size("lon")
    lat = lax.axis_size("lat")
    hop = [(i * lon + j, i * lon + (j + (1 if i % 2 == 0 else -1)) % lon) for i in range(lat) for j in range(lon)]
    back = [(target, source) for source, target in hop]
    siblings = [(i, i ^ 1) for i in range(lat)]
    pos_pair = jnp.concatenate([tile_pos, lax.ppermute(tile_pos, "lat", siblings)], axis=0)
    pos_far = lax.ppermute(pos_pair, ("lat", "lon"), back)
    shell, inputs = pl.pallas_call(
        shell_kernel,
        out_shape=(pltpu.VMEM((KPAD, PAY), BF16), pltpu.VMEM((A_DEV, KPAD, TT), BF16)),
        in_specs=[smem, smem, vmem, vmem],
        out_specs=(vmem, vmem),
        scratch_shapes=[
            pltpu.VMEM((2, A_DEV * CIN, HALF), F32),
            pltpu.VMEM((2, A_DEV * CIN, HALF), F32),
            pltpu.VMEM((KPAD, PAY), F32),
        ],
        name="shell",
    )(tile_pos, valid_rows, x_tiles[0].transpose(1, 0, 2), jnp.asarray(shell_cells()))
    shell, pos_far = lax.optimization_barrier((shell, pos_far))
    same_core = [[i for i in range(c, lat, 2)] for c in range(2)]
    mine = lax.all_to_all(
        jnp.broadcast_to(shell[None], (GROUP, KPAD, PAY)), "lat", 0, 0, axis_index_groups=same_core, tiled=True
    )
    theirs = lax.ppermute(mine, "lat", siblings)
    side, band, give = pl.pallas_call(
        pick_kernel,
        out_shape=(
            pltpu.VMEM((2, A_DEV * STRIP, KPAD), BF16),
            pltpu.VMEM((2 * A_DEV, PIECE, KPAD), BF16),
            pltpu.VMEM((2, A_DEV * STRIP, KPAD), BF16),
        ),
        in_specs=[smem] * 2 + [vmem] * 3,
        out_specs=(vmem, vmem, vmem),
        scratch_shapes=[
            pltpu.VMEM((16, PAY), F32),
            pltpu.VMEM((64, HALF), F32),
            pltpu.VMEM((64, HALF), jnp.int32),
            pltpu.SMEM((64, HALF), jnp.int32),
            pltpu.SemaphoreType.DMA,
            pltpu.VMEM((8, STRIP, 256), jnp.int32),
        ],
        compiler_params=pltpu.CompilerParams(vmem_limit_bytes=16 << 20),
        name="pick",
    )(tile_pos, pos_far, on_chip(mine), on_chip(theirs), jnp.asarray(strip_sources()))
    near = lax.ppermute(give, ("lat", "lon"), hop)
    swap = lax.ppermute(near, "lat", siblings)

    cells = A_DEV * TT
    out_tiles, own, send = pl.pallas_call(
        main_kernel,
        out_shape=(
            jax.ShapeDtypeStruct((A_DEV, C, TT), BF16),
            pltpu.VMEM((CHUNKS, 24, HALF), F32),
            pltpu.VMEM((CHUNKS, 24, HALF), BF16),
        ),
        in_specs=[smem] + [vmem] * 11,
        out_specs=(vmem, vmem, vmem),
        scratch_shapes=[
            pltpu.VMEM((KPAD, 256), BF16),
            pltpu.VMEM((2, 56, HALF), F32),
            pltpu.VMEM((1, 256), F32),
            pltpu.VMEM((256, HB * HALF), F32),
            pltpu.VMEM((HB * HALF, 256), BF16),
            pltpu.VMEM((HB * HALF, 256), BF16),
            pltpu.VMEM((2, A_DEV * PROWS * PITCH, HALF), F32),
            pltpu.VMEM((2, cells, HALF), F32),
            pltpu.VMEM((2, 56, HALF), F32),
            pltpu.VMEM((cells, HALF), F32),
            pltpu.VMEM((256, cells), BF16),
            pltpu.VMEM((256, cells), BF16),
            pltpu.VMEM((HID, cells), BF16),
            pltpu.VMEM((HID, cells), BF16),
            pltpu.VMEM((256, TT), F32),
            pltpu.VMEM((2, cells, HALF), F32),
            pltpu.VMEM((C, HB * HALF), F32),
            pltpu.VMEM((C, HB * HALF), F32),
        ],
        compiler_params=pltpu.CompilerParams(vmem_limit_bytes=32 << 20),
        name="block",
    )(in_hbm(valid_rows), side, band, on_chip(near), on_chip(swap), inputs, stem_w, dw_kernel.T, in_hbm(norm_gain.reshape(1, C)), w_in, w_out.T, cotangent[0])

    arrived = lax.ppermute(send, "lat", siblings)
    chip_sum = (own + arrived.astype(F32)).astype(BF16)
    every = [[i * lon + j for i in range(c, lat, 2) for j in range(lon)] for c in range(2)]
    part = lax.all_to_all(chip_sum, ("lat", "lon"), 0, 0, axis_index_groups=every, tiled=True)
    part = jnp.sum(part.astype(F32), axis=0)
    whole = part.astype(BF16)
    spread = jnp.broadcast_to(whole[None], (CHUNKS, 24, HALF))
    spread = lax.all_to_all(spread, ("lat", "lon"), 0, 0, axis_index_groups=every, tiled=True)
    other = lax.ppermute(spread, "lat", siblings)
    win, wout, ker, gain = pl.pallas_call(
        final_kernel,
        out_shape=(
            jax.ShapeDtypeStruct((C, HID), F32),
            jax.ShapeDtypeStruct((C, HID), F32),
            jax.ShapeDtypeStruct((KW * KW, C), F32),
            jax.ShapeDtypeStruct((1, C), F32),
        ),
        in_specs=[vmem, vmem],
        out_specs=(vmem, vmem, vmem, vmem),
        scratch_shapes=[pltpu.VMEM((56, 256), F32)],
        compiler_params=pltpu.CompilerParams(vmem_limit_bytes=8 << 20),
        name="finish",
    )(on_chip(spread), on_chip(other))
    return out_tiles[None], win, wout.T, ker.T, gain.reshape(C)


def solution(mesh):
    tiles = P("lon", "lat", None, None)
    in_specs = (tiles, P("lon", "lat"), P("lon", "lat"), P(), P(), P(), P(), P(), tiles)
    out_specs = (tiles, P(), P(), P(), P())
    return jax.shard_map(body, mesh=mesh, in_specs=in_specs, out_specs=out_specs, check_vma=False)
```
